512 devices in a mesh: gx: 64 (over y, z), gy: 8 (over x, core).
Axes of the slice: x: 4, y: 4, z: 16, core: 2. Of those that a mesh axis runs over, the one named last changes fastest.
Arguments:
- thermal_field: float32 [8, 256, 8192], P(None, 'gy', 'gx'), may hold values from -6 to 6
- material_state: int32 [8, 256, 8192], P(None, 'gy', 'gx'), may hold values from 0 to 2
- beam_path_indicator: int32 [8, 256, 8192], P(None, 'gy', 'gx'), may hold values 0 or 1
- state_diffusivity_table: float32 [3], replicated, may hold values from 0.5 to 2
Outputs:
- new_temperature: float32 [8, 256, 8192], P(None, 'gy', 'gx')
The draws below stay inside these ranges and needn't reach their ends.
All inputs are finite; a program needn't handle non-finite values. No bound on the sum of `beam_path_indicator` on one device may be relied on, other than what follows from the above.
Results may differ from the reference program's by a relative error of at most 0.02.
Values sent between devices are 32-bit elements; how exact they have to be, the bound alone decides.
A program may use at most 64 MiB of HBM per device.

```python
import math
import jax
import jax.numpy as jnp
from jax import lax

NZ = 8
NX = 8192
NY = 256


def draw_thermal_field(key, part):
    key_rough = jax.random.fold_in(key, 11)
    return jax.random.truncated_normal(key_rough, -6.0, 6.0, (NZ, NY, NX), jnp.float32)


def touch_ends(result, rng, smallest, high):
    dims = result.shape
    spot = [jax.random.randint(jax.random.fold_in(rng, axis), (), 0, dims[axis]) for axis in range(len(dims))]
    result = result.at[tuple(spot)].set(smallest)
    longest = dims.index(max(dims))
    spot[longest] = (spot[longest] + 1) % dims[longest]
    return result.at[tuple(spot)].set(high)


def setup_inputs(seed: int = 0) -> dict:
    key_list = jax.random.split(jax.random.key(seed), 5)
    return {
        "thermal_field": draw_thermal_field(jax.random.fold_in(key_list[4], 71), 0),
        "material_state": touch_ends(jax.random.randint(key_list[1], (NZ, NY, NX), 0, 3), jax.random.fold_in(key_list[1], 1), 0, 2).astype(jnp.int32),
        "beam_path_indicator": touch_ends((jax.random.randint(key_list[2], (NZ, NY, NX), 0, 8) < 1).astype(jnp.int32), jax.random.fold_in(key_list[2], 1), 0, 1),
        "state_diffusivity_table": jnp.clip(jnp.exp(jax.random.uniform(key_list[3], (3,), jnp.float32, math.log(0.5), math.log(2.0))), 0.5, 2.0),
    }


ratio_x = 65536.0
transverse_step_quotient = 1.0
energy_input_factor = 4.0


def face_value(first, second):
    return 2.0 * first * second / (first + second)


def summed_spreading(temp_pad, cond_pad, axis):
    count = temp_pad.shape[axis]
    upper_temp = lax.slice_in_dim(temp_pad, 1, count, axis=axis)
    lower_temp = lax.slice_in_dim(temp_pad, 0, count - 1, axis=axis)
    upper_cond = lax.slice_in_dim(cond_pad, 1, count, axis=axis)
    lower_cond = lax.slice_in_dim(cond_pad, 0, count - 1, axis=axis)
    flux = face_value(upper_cond, lower_cond) * (upper_temp - lower_temp)
    return lax.slice_in_dim(flux, 1, count - 1, axis=axis) - lax.slice_in_dim(flux, 0, count - 2, axis=axis)


def thomas_solve(lower, diag, upper, known_vector):
    def forward(carry, row):
        prev_c, prev_d = carry
        low, mid, upp, side = row
        denom = mid - low * prev_c
        new_c = upp / denom
        new_d = (side - low * prev_d) / denom
        return (new_c, new_d), (new_c, new_d)

    zero_boundary = jnp.zeros(known_vector.shape[1:], known_vector.dtype)
    _, (mod_c, mod_d) = lax.scan(forward, (zero_boundary, zero_boundary), (lower, diag, upper, known_vector))

    def backward(nxt, row):
        cval, dval = row
        value = dval - cval * nxt
        return value, value

    _, answered_pencils = lax.scan(backward, zero_boundary, (mod_c, mod_d), reverse=True)
    return answered_pencils


def reference(thermal_field, material_state, beam_path_indicator, state_diffusivity_table):
    local_diffusivity_coefficient = state_diffusivity_table[material_state]
    spacing_second_axis = ((0, 0), (1, 1), (0, 0))
    spacing_third_axis = ((1, 1), (0, 0), (0, 0))
    spread_second_axis = summed_spreading(jnp.pad(thermal_field, spacing_second_axis), jnp.pad(local_diffusivity_coefficient, spacing_second_axis), 1)
    spread_third_axis = summed_spreading(jnp.pad(thermal_field, spacing_third_axis), jnp.pad(local_diffusivity_coefficient, spacing_third_axis), 0)
    known_vector = thermal_field + transverse_step_quotient * spread_second_axis + transverse_step_quotient * spread_third_axis + energy_input_factor * beam_path_indicator.astype(jnp.float32)
    cond_x = jnp.pad(local_diffusivity_coefficient, ((0, 0), (0, 0), (1, 1)))
    face_x = face_value(cond_x[:, :, :-1], cond_x[:, :, 1:])
    lower = -ratio_x * face_x[:, :, :-1]
    upper = -ratio_x * face_x[:, :, 1:]
    diag = 1.0 - lower - upper
    pencil_rows = thermal_field.shape[0] * thermal_field.shape[1]
    pencil_count = thermal_field.shape[2]

    def to_lines(field):
        return field.reshape(pencil_rows, pencil_count).T

    answered_pencils = thomas_solve(to_lines(lower), to_lines(diag), to_lines(upper), to_lines(known_vector))
    return answered_pencils.T.reshape(thermal_field.shape)
```

```python
import jax
import jax.numpy as jnp
from jax import lax
from jax.experimental import pallas as pl
from jax.experimental.pallas import tpu as pltpu
from jax.sharding import PartitionSpec as P

MESH = pl.DeviceIdType.MESH
RATIO = 65536.0
NSEG = 64
NGY = 8
NEAR = (-3, -2, -1, 1, 2, 3, 4)
FAR = (4, 12, 20, 28, 36, 44, 52, 60)


def face(a, b):
    return 2.0 * a * b / (a + b)


def split(x):
    high = 4097.0 * x
    high = high - (high - x)
    return high, x - high


def exact_face(a, b):
    above, below = 2.0 * a * b, a + b
    q = above / below
    (qh, ql), (bh, bl) = split(q), split(below)
    p = q * below
    error = ((qh * bh - p) + qh * bl + ql * bh) + ql * bl
    return q + ((above - p) - error) / below


def shunt_of(left, right):
    once = 1.0 + left
    diag = once + right
    part = diag - once
    return (once - left) - ((once - (diag - part)) + (right - part))


def combine(a, b):
    ab, aal, abe, as1, as2 = a
    bb, bal, bbe, bs1, bs2 = b
    shunt = abe + bal
    r = 1.0 / (ab + bb + shunt)
    pa, pb = ab * r, bb * r
    s = as2 + bs1
    return (pa * bb, aal + pa * shunt, bbe + pb * shunt, as1 + pa * s, bs2 + pb * s)


def build(g, shunts, lo, hi):
    if hi - lo == 1:
        return (g[lo], shunts[lo], None), []
    half = 1
    while half * 2 < hi - lo:
        half *= 2
    mid = lo + half
    (ab, aal, abe), left = build(g, shunts, lo, mid)
    (bb, bal, bbe), right = build(g, shunts, mid, hi)
    shunt = bal if abe is None else bal + abe
    r = 1.0 / (ab + bb + shunt)
    pa, pb = ab * r, bb * r
    al = aal + pa * shunt
    be = pb * shunt if bbe is None else bbe + pb * shunt
    return (pa * bb, al, be), left + right + [(mid, lo, hi, pa, pb, r)]


def kernel(
    t_hbm, m_hbm, b_hbm, table, out_ref,
    tv, mv, bv, cv, fv, trans, pq, edge, elim, hs, hr, xs, xr, own, mine, near, mid, far,
    load_sem, hs_sem, hr_sem, xs_sem, xr_sem, ns_sem, nr_sem, fs_sem, fr_sem,
):
    gx, gy = lax.axis_index("gx"), lax.axis_index("gy")

    loads = [
        pltpu.make_async_copy(src, dst, load_sem.at[k])
        for k, (src, dst) in enumerate(((m_hbm, mv), (t_hbm, tv), (b_hbm, bv)))
    ]
    for load in loads:
        load.start()

    def seg(offset):
        return {"gx": lax.rem(gx + (offset % NSEG), NSEG)}

    def side(offset):
        return {"gy": lax.rem(gy + (offset % NGY), NGY)}

    barrier = pltpu.get_barrier_semaphore()
    senders = [seg(o) for o in sorted(set(o % NSEG for o in NEAR + FAR))] + [side(1), side(-1)]
    for device in senders:
        pl.semaphore_signal(barrier, inc=1, device_id=device, device_id_type=MESH)

    loads[0].wait()
    t0, t1, t2 = table[0], table[1], table[2]
    m = mv[...]
    cv[...] = jnp.where(m == 0, t0, jnp.where(m == 1, t1, t2))
    loads[1].wait()
    hs[0, 0] = tv[pl.ds(0, 8, stride=32), :]
    hs[0, 1] = cv[pl.ds(0, 8, stride=32), :]
    hs[1, 0] = tv[pl.ds(31, 8, stride=32), :]
    hs[1, 1] = cv[pl.ds(31, 8, stride=32), :]
    for h in range(2):
        trans[h] = cv[128 * h : 128 * h + 128, :].T
        xs[0, h : h + 1, :] = trans[h, 0:1, :]
        xs[1, h : h + 1, :] = trans[h, 127:128, :]

    pl.semaphore_wait(barrier, len(senders))
    halo = [
        pltpu.make_async_remote_copy(
            src_ref=hs.at[k], dst_ref=hr.at[1 - k], send_sem=hs_sem.at[k], recv_sem=hr_sem.at[1 - k],
            device_id=side(2 * k - 1), device_id_type=MESH,
        )
        for k in range(2)
    ]
    halo_x = [
        pltpu.make_async_remote_copy(
            src_ref=xs.at[k], dst_ref=xr.at[1 - k], send_sem=xs_sem.at[k], recv_sem=xr_sem.at[1 - k],
            device_id=seg(2 * k - 1), device_id_type=MESH,
        )
        for k in range(2)
    ]
    for copy in halo + halo_x:
        copy.start()

    shape = (2, 8, 128)
    row = lax.broadcasted_iota(jnp.int32, shape, 1)

    tables = [jnp.full((8, 128), t, jnp.float32) for t in (t0, t1, t2)]
    faces = {}
    for i in range(3):
        for j in range(i, 3):
            faces[i, j] = faces[j, i] = RATIO * exact_face(tables[i], tables[j])[0:1, :]

    def joint(a, b):
        b0, b1 = b == t0, b == t1
        rows = [jnp.where(b0, faces[i, 0], jnp.where(b1, faces[i, 1], faces[i, 2])) for i in range(3)]
        return jnp.where(a == t0, rows[0], jnp.where(a == t1, rows[1], rows[2]))

    def piece(j):
        return jnp.stack([trans[h, pl.ds(j, 8, stride=16), :] for h in range(2)])

    cond = [piece(j) for j in range(16)]
    cond.append(pltpu.roll(cond[0], 7, 1))
    g = [joint(cond[j], cond[j + 1]) for j in range(16)]
    last = row == 7
    shunts = [jnp.where(row == 0, 0.0, shunt_of(pltpu.roll(g[15], 1, 1), g[0]))]
    shunts += [shunt_of(g[j - 1], g[j]) for j in range(1, 16)]
    (cb, cal, cbe), steps = build(g, shunts, 0, 15)
    cbe = cbe + jnp.where(last, 0.0, shunts[15])
    r15 = 1.0 / (cb + cbe + g[15])
    pa15, pb15 = cb * r15, g[15] * r15
    b = jnp.where(last, cb, pa15 * g[15])
    al = jnp.where(last, cal, cal + pa15 * cbe)
    be = jnp.where(last, cbe, pb15 * cbe)
    levels = []
    for step in (1, 2, 4):
        bb, bal, bbe = (pltpu.roll(v, 8 - step, 1) for v in (b, al, be))
        shunt = be + bal
        r = 1.0 / (b + bb + shunt)
        pa, pb = b * r, bb * r
        b, al, be = pa * bb, al + pa * shunt, bbe + pb * shunt
        levels.append((step, pa, pb, r))
    for h in range(2):
        own[0, h : h + 1, :] = b[h, 0:1, :]
        own[1, h : h + 1, :] = al[h, 0:1, :]
        own[2, h : h + 1, :] = be[h, 0:1, :]
        own[5, h : h + 1, :] = g[0][h, 0:1, :]
        own[6, h : h + 1, :] = g[14][h, 7:8, :]

    def spread(value, step):
        if step == 4:
            return jnp.broadcast_to(value[:, 0:1, :], shape)
        if step == 2:
            return jnp.where(row < 4, value[:, 0:1, :], value[:, 4:5, :])
        return jnp.where(row % 2 == 0, value, pltpu.roll(value, 1, 1))

    def descend(left, right, sources):
        for k, (step, pa, pb, _) in reversed(list(enumerate(levels))):
            centre = pa * left + pb * right
            if sources is not None:
                centre = centre + sources[0][k]
            centre = spread(centre, step)
            low = (row // step) % 2 == 0
            left, right = jnp.where(low, left, centre), jnp.where(low, centre, right)
        end = pa15 * left + pb15 * right
        if sources is not None:
            end = end + sources[1]
        values = {0: left, 15: jnp.where(last, right, end)}
        for node, lo, hi, pa, pb, _ in reversed(steps):
            values[node] = pa * values[lo] + pb * values[hi]
            if sources is not None:
                values[node] = values[node] + sources[2][node]
        return [values[j] for j in range(16)]

    one, zero = jnp.ones(shape, jnp.float32), jnp.zeros(shape, jnp.float32)
    for j, value in enumerate(descend(one, zero, None)):
        pq[0, j] = value
    for j, value in enumerate(descend(zero, one, None)):
        pq[1, j] = value
    for k, (_, _, _, _, _, r) in enumerate(steps):
        elim[k] = r

    loads[2].wait()
    line = lax.broadcasted_iota(jnp.int32, (32, 128), 0)
    below = None
    for z in range(8):
        here = slice(32 * z, 32 * z + 32)
        tz, cz = tv[here, :], cv[here, :]
        flux = jnp.where(line < 31, face(cz, pltpu.roll(cz, 31, 0)) * (pltpu.roll(tz, 31, 0) - tz), 0.0)
        value = tz + (flux - pltpu.roll(flux, 1, 0)) + 4.0 * bv[here, :].astype(jnp.float32)
        if below is not None:
            value = value - below
        if z < 7:
            above = slice(32 * z + 32, 32 * z + 64)
            below = face(cz, cv[above, :]) * (tv[above, :] - tz)
            value = value + below
        fv[here, :] = value

    for copy in halo:
        copy.wait_recv()
    low, high = pl.ds(0, 8, stride=32), pl.ds(31, 8, stride=32)
    flux = face(hs[1, 1], hr[1, 1]) * (hr[1, 0] - hs[1, 0])
    fv[high, :] = fv[high, :] + jnp.where(gy < NGY - 1, flux, 0.0)
    flux = face(hs[0, 1], hr[0, 1]) * (hs[0, 0] - hr[0, 0])
    fv[low, :] = fv[low, :] - jnp.where(gy > 0, flux, 0.0)
    for h in range(2):
        trans[h] = fv[128 * h : 128 * h + 128, :].T

    first, second = zero, zero
    for j in range(16):
        f = piece(j)
        first, second = first + pq[0, j] * f, second + pq[1, j] * f
    for h in range(2):
        own[3, h : h + 1, :] = jnp.sum(first[h], axis=0, keepdims=True)
        own[4, h : h + 1, :] = jnp.sum(second[h], axis=0, keepdims=True)

    for copy in halo_x:
        copy.wait_recv()
    ob, oal, obe, os1, os2, first_g, last_g = (own[k] for k in range(7))
    og = jnp.where(gx < NSEG - 1, joint(xs[1], xr[1]), 0.0)
    oal = oal + shunt_of(jnp.where(gx > 0, joint(xr[0], xs[0]), 0.0), first_g)
    obe = obe + shunt_of(last_g, og)
    r = 1.0 / (ob + obe + og)
    pa, pb = ob * r, og * r
    whole = (pa * og, oal + pa * obe, pb * obe, os1 + pa * os2, pb * os2)
    for k in range(5):
        mine[k] = whole[k]
    near_copies = [
        pltpu.make_async_remote_copy(
            src_ref=mine, dst_ref=near.at[k], send_sem=ns_sem.at[k], recv_sem=nr_sem.at[k],
            device_id=seg(-o), device_id_type=MESH,
        )
        for k, o in enumerate(NEAR)
    ]
    for k in (6, 5, 0, 4, 1, 3, 2):
        near_copies[k].start()

    steps = [(node, lo, hi, pa, pb, elim[k]) for k, (node, lo, hi, pa, pb, _) in enumerate(steps)]
    f = [piece(j) for j in range(16)]
    ends = {(j, j + 1): (f[j], None) for j in range(15)}
    inner = {}
    for node, lo, hi, pa, pb, r in steps:
        a, c = ends[lo, node], ends[node, hi]
        s = c[0] if a[1] is None else a[1] + c[0]
        inner[node] = s * r
        ends[lo, hi] = (a[0] + pa * s, pb * s if c[1] is None else c[1] + pb * s)
    s1, s2 = ends[0, 15]
    s2 = s2 + f[15]
    at_end = r15 * s2
    s1, s2 = jnp.where(last, s1, s1 + pa15 * s2), jnp.where(last, s2, pb15 * s2)
    middle = []
    for step, pa, pb, r in levels:
        bs1, bs2 = pltpu.roll(s1, 8 - step, 1), pltpu.roll(s2, 8 - step, 1)
        s = s2 + bs1
        middle.append(s * r)
        s1, s2 = s1 + pa * s, bs2 + pb * s
    for j, value in enumerate(descend(zero, zero, (middle, at_end, inner))):
        pq[2, j] = value

    for copy in near_copies:
        copy.wait_recv()
    item = {o: tuple(near[k, i] for i in range(5)) for k, o in enumerate(NEAR)}
    item[0] = whole
    ahead = combine(combine(item[1], item[2]), combine(item[3], item[4]))
    behind = combine(item[-3], item[-2])
    behind_own = combine(behind, combine(item[-1], item[0]))
    behind = combine(behind, item[-1])
    window = combine(behind_own, ahead)
    for k in range(5):
        mid[0, k] = ahead[k]
        mid[1, k] = window[k]
        mid[2, k] = behind_own[k]
    far_copies = [
        pltpu.make_async_remote_copy(
            src_ref=mid.at[0 if k == 0 else 2 if k == 7 else 1], dst_ref=far.at[k],
            send_sem=fs_sem.at[k], recv_sem=fr_sem.at[k],
            device_id=seg(-o), device_id_type=MESH,
        )
        for k, o in enumerate(FAR)
    ]
    for k in (3, 4, 2, 5, 1, 6, 0, 7):
        far_copies[k].start()
    for copy in far_copies:
        copy.wait_recv()
    chain = [ahead] + [tuple(far[k, i] for i in range(5)) for k in range(8)] + [behind]
    while len(chain) > 1:
        chain = [combine(*chain[k : k + 2]) if k + 1 < len(chain) else chain[k] for k in range(0, len(chain), 2)]
    _, right_g, left_g, right_s, left_s = chain[0]

    r = og / (og + right_g)
    end_g, end_s = obe + r * right_g, os2 + r * right_s
    r = 1.0 / (ob + end_g)
    start = (os1 + left_s + ob * r * end_s) / (oal + left_g + ob * r * end_g)
    end = r * (ob * start + end_s)
    start = jnp.stack([jnp.broadcast_to(start[h : h + 1, :], (8, 128)) for h in range(2)])
    end = jnp.stack([jnp.broadcast_to(end[h : h + 1, :], (8, 128)) for h in range(2)])
    for j in range(16):
        value = pq[2, j] + pq[0, j] * start + pq[1, j] * end
        for h in range(2):
            trans[h, pl.ds(j, 8, stride=16), :] = value[h]
    for h in range(2):
        out_ref[128 * h : 128 * h + 128, :] = trans[h].T

    for copy in halo + halo_x + near_copies + far_copies:
        copy.wait_send()


def local(thermal_field, material_state, beam_path_indicator, state_diffusivity_table):
    f32 = jnp.float32
    flat = (256, 128)
    hbm = pl.BlockSpec(memory_space=pltpu.HBM)
    dma = pltpu.SemaphoreType.DMA
    out = pl.pallas_call(
        kernel,
        out_shape=jax.ShapeDtypeStruct(flat, f32),
        in_specs=[hbm, hbm, hbm, pl.BlockSpec(memory_space=pltpu.SMEM)],
        out_specs=pl.BlockSpec(memory_space=pltpu.VMEM),
        scratch_shapes=[
            pltpu.VMEM(flat, f32),
            pltpu.VMEM(flat, jnp.int32),
            pltpu.VMEM(flat, jnp.int32),
            pltpu.VMEM(flat, f32),
            pltpu.VMEM(flat, f32),
            pltpu.VMEM((2, 128, 128), f32),
            pltpu.VMEM((3, 16, 2, 8, 128), f32),
            pltpu.VMEM((8, 128), f32),
            pltpu.VMEM((14, 2, 8, 128), f32),
            pltpu.VMEM((2, 2, 8, 128), f32),
            pltpu.VMEM((2, 2, 8, 128), f32),
            pltpu.VMEM((2, 2, 128), f32),
            pltpu.VMEM((2, 2, 128), f32),
            pltpu.VMEM((7, 2, 128), f32),
            pltpu.VMEM((5, 2, 128), f32),
            pltpu.VMEM((len(NEAR), 5, 2, 128), f32),
            pltpu.VMEM((3, 5, 2, 128), f32),
            pltpu.VMEM((len(FAR), 5, 2, 128), f32),
            dma((3,)),
            dma((2,)),
            dma((2,)),
            dma((2,)),
            dma((2,)),
            dma((len(NEAR),)),
            dma((len(NEAR),)),
            dma((len(FAR),)),
            dma((len(FAR),)),
        ],
        compiler_params=pltpu.CompilerParams(collective_id=0, has_side_effects=True),
        name="adi_x",
    )(
        thermal_field.reshape(flat),
        material_state.reshape(flat),
        beam_path_indicator.reshape(flat),
        state_diffusivity_table,
    )
    return out.reshape(thermal_field.shape)


def solution(mesh):
    in_specs = (P(None, "gy", "gx"), P(None, "gy", "gx"), P(None, "gy", "gx"), P())
    out_specs = P(None, "gy", "gx")
    return jax.shard_map(local, mesh=mesh, in_specs=in_specs, out_specs=out_specs, check_vma=False)
```

```python
import jax
import jax.numpy as jnp
from jax import lax
from jax.experimental import pallas as pl
from jax.experimental.pallas import tpu as pltpu
from jax.sharding import PartitionSpec as P

MESH = pl.DeviceIdType.MESH
RATIO = 65536.0
NSEG = 64
NGY = 8
NEAR = (-3, -2, -1, 1, 2, 3, 4)
GREET = (-2, -1, 1, 2, 16, 32, 48)
FAR = (4, 12, 20, 28, 36, 44, 52, 60)


def face(a, b):
    return 2.0 * a * b / (a + b)


def split(x):
    high = 4097.0 * x
    high = high - (high - x)
    return high, x - high


def exact_face(a, b):
    above, below = 2.0 * a * b, a + b
    q = above / below
    (qh, ql), (bh, bl) = split(q), split(below)
    p = q * below
    error = ((qh * bh - p) + qh * bl + ql * bh) + ql * bl
    return q + ((above - p) - error) / below


def shunt_of(left, right):
    once = 1.0 + left
    diag = once + right
    part = diag - once
    return (once - left) - ((once - (diag - part)) + (right - part))


def combine(a, b):
    ab, aal, abe, as1, as2 = a
    bb, bal, bbe, bs1, bs2 = b
    shunt = abe + bal
    r = 1.0 / (ab + bb + shunt)
    pa, pb = ab * r, bb * r
    s = as2 + bs1
    return (pa * bb, aal + pa * shunt, bbe + pb * shunt, as1 + pa * s, bs2 + pb * s)


def build(g, shunts, lo, hi):
    if hi - lo == 1:
        return (g[lo], shunts[lo], None), []
    half = 1
    while half * 2 < hi - lo:
        half *= 2
    mid = lo + half
    (ab, aal, abe), left = build(g, shunts, lo, mid)
    (bb, bal, bbe), right = build(g, shunts, mid, hi)
    shunt = bal if abe is None else bal + abe
    r = 1.0 / (ab + bb + shunt)
    pa, pb = ab * r, bb * r
    al = aal + pa * shunt
    be = pb * shunt if bbe is None else bbe + pb * shunt
    return (pa * bb, al, be), left + right + [(mid, lo, hi, pa, pb, r)]


def kernel(
    t_hbm, m_hbm, b_hbm, table, out_ref,
    tv, mv, bv, cv, fv, trans, pq, elim, hs, hr, xs, xr, own, mine, near, mid, far,
    load_sem, hs_sem, hr_sem, xs_sem, xr_sem, ns_sem, nr_sem, fs_sem, fr_sem, word_sem,
):
    gx, gy = lax.axis_index("gx"), lax.axis_index("gy")

    loads = [
        pltpu.make_async_copy(src, dst, load_sem.at[k])
        for k, (src, dst) in enumerate(((m_hbm, mv), (t_hbm, tv), (b_hbm, bv)))
    ]
    for load in loads:
        load.start()

    def seg(offset):
        return {"gx": lax.rem(gx + (offset % NSEG), NSEG)}

    def side(offset):
        return {"gy": lax.rem(gy + (offset % NGY), NGY)}

    barrier = pltpu.get_barrier_semaphore()
    greeted = [side(1), side(-1)] + [seg(o) for o in GREET]
    for device in greeted:
        pl.semaphore_signal(barrier, inc=1, device_id=device, device_id_type=MESH)

    t0, t1, t2 = table[0], table[1], table[2]

    def conductivity(m):
        return jnp.where(m == 0, t0, jnp.where(m == 1, t1, t2))

    low, high = pl.ds(0, 8, stride=32), pl.ds(31, 8, stride=32)
    loads[0].wait()
    hs[0, 1] = conductivity(mv[low, :])
    hs[1, 1] = conductivity(mv[high, :])
    loads[1].wait()
    hs[0, 0] = tv[low, :]
    hs[1, 0] = tv[high, :]

    pl.semaphore_wait(barrier, len(greeted))
    halo = [
        pltpu.make_async_remote_copy(
            src_ref=hs.at[k], dst_ref=hr.at[1 - k], send_sem=hs_sem.at[k], recv_sem=hr_sem.at[1 - k],
            device_id=side(2 * k - 1), device_id_type=MESH,
        )
        for k in range(2)
    ]
    for copy in halo:
        copy.start()
    for k in range(2):
        pl.semaphore_signal(word_sem.at[k], inc=1, device_id=seg(4 * k - 2), device_id_type=MESH)

    cv[...] = conductivity(mv[...])
    for h in range(2):
        trans[h] = cv[128 * h : 128 * h + 128, :].T
        xs[0, h : h + 1, :] = trans[h, 0:1, :]
        xs[1, h : h + 1, :] = trans[h, 127:128, :]
    halo_x = [
        pltpu.make_async_remote_copy(
            src_ref=xs.at[k], dst_ref=xr.at[1 - k], send_sem=xs_sem.at[k], recv_sem=xr_sem.at[1 - k],
            device_id=seg(2 * k - 1), device_id_type=MESH,
        )
        for k in range(2)
    ]
    for copy in halo_x:
        copy.start()

    shape = (2, 8, 128)
    row = lax.broadcasted_iota(jnp.int32, shape, 1)

    tables = [jnp.full((8, 128), t, jnp.float32) for t in (t0, t1, t2)]
    faces = {}
    for i in range(3):
        for j in range(i, 3):
            faces[i, j] = faces[j, i] = RATIO * exact_face(tables[i], tables[j])[0:1, :]

    def joint(a, b):
        b0, b1 = b == t0, b == t1
        rows = [jnp.where(b0, faces[i, 0], jnp.where(b1, faces[i, 1], faces[i, 2])) for i in range(3)]
        return jnp.where(a == t0, rows[0], jnp.where(a == t1, rows[1], rows[2]))

    def piece(j):
        return jnp.stack([trans[h, pl.ds(j, 8, stride=16), :] for h in range(2)])

    cond = [piece(j) for j in range(16)]
    cond.append(pltpu.roll(cond[0], 7, 1))
    g = [joint(cond[j], cond[j + 1]) for j in range(16)]
    last = row == 7
    shunts = [jnp.where(row == 0, 0.0, shunt_of(pltpu.roll(g[15], 1, 1), g[0]))]
    shunts += [shunt_of(g[j - 1], g[j]) for j in range(1, 16)]
    (cb, cal, cbe), steps = build(g, shunts, 0, 15)
    cbe = cbe + jnp.where(last, 0.0, shunts[15])
    r15 = 1.0 / (cb + cbe + g[15])
    pa15, pb15 = cb * r15, g[15] * r15
    b = jnp.where(last, cb, pa15 * g[15])
    al = jnp.where(last, cal, cal + pa15 * cbe)
    be = jnp.where(last, cbe, pb15 * cbe)
    levels = []
    for step in (1, 2, 4):
        bb, bal, bbe = (pltpu.roll(v, 8 - step, 1) for v in (b, al, be))
        shunt = be + bal
        r = 1.0 / (b + bb + shunt)
        pa, pb = b * r, bb * r
        b, al, be = pa * bb, al + pa * shunt, bbe + pb * shunt
        levels.append((step, pa, pb, r))
    for h in range(2):
        own[0, h : h + 1, :] = b[h, 0:1, :]
        own[1, h : h + 1, :] = al[h, 0:1, :]
        own[2, h : h + 1, :] = be[h, 0:1, :]
        own[5, h : h + 1, :] = g[0][h, 0:1, :]
        own[6, h : h + 1, :] = g[14][h, 7:8, :]

    def spread(value, step):
        if step == 4:
            return jnp.broadcast_to(value[:, 0:1, :], shape)
        if step == 2:
            return jnp.where(row < 4, value[:, 0:1, :], value[:, 4:5, :])
        return jnp.where(row % 2 == 0, value, pltpu.roll(value, 1, 1))

    def descend(left, right, sources):
        for k, (step, pa, pb, _) in reversed(list(enumerate(levels))):
            centre = pa * left + pb * right
            if sources is not None:
                centre = centre + sources[0][k]
            centre = spread(centre, step)
            low = (row // step) % 2 == 0
            left, right = jnp.where(low, left, centre), jnp.where(low, centre, right)
        end = pa15 * left + pb15 * right
        if sources is not None:
            end = end + sources[1]
        values = {0: left, 15: jnp.where(last, right, end)}
        for node, lo, hi, pa, pb, _ in reversed(steps):
            values[node] = pa * values[lo] + pb * values[hi]
            if sources is not None:
                values[node] = values[node] + sources[2][node]
        return [values[j] for j in range(16)]

    one, zero = jnp.ones(shape, jnp.float32), jnp.zeros(shape, jnp.float32)
    for j, value in enumerate(descend(one, zero, None)):
        pq[0, j] = value
    for j, value in enumerate(descend(zero, one, None)):
        pq[1, j] = value
    for k, (_, _, _, _, _, r) in enumerate(steps):
        elim[k] = r

    loads[2].wait()
    line = lax.broadcasted_iota(jnp.int32, (32, 128), 0)
    below = None
    for z in range(8):
        here = slice(32 * z, 32 * z + 32)
        tz, cz = tv[here, :], cv[here, :]
        flux = jnp.where(line < 31, face(cz, pltpu.roll(cz, 31, 0)) * (pltpu.roll(tz, 31, 0) - tz), 0.0)
        value = tz + (flux - pltpu.roll(flux, 1, 0)) + 4.0 * bv[here, :].astype(jnp.float32)
        if below is not None:
            value = value - below
        if z < 7:
            above = slice(32 * z + 32, 32 * z + 64)
            below = face(cz, cv[above, :]) * (tv[above, :] - tz)
            value = value + below
        fv[here, :] = value

    for copy in halo:
        copy.wait_recv()
    flux = face(hs[1, 1], hr[1, 1]) * (hr[1, 0] - hs[1, 0])
    fv[high, :] = fv[high, :] + jnp.where(gy < NGY - 1, flux, 0.0)
    flux = face(hs[0, 1], hr[0, 1]) * (hs[0, 0] - hr[0, 0])
    fv[low, :] = fv[low, :] - jnp.where(gy > 0, flux, 0.0)
    for h in range(2):
        trans[h] = fv[128 * h : 128 * h + 128, :].T

    first, second = zero, zero
    for j in range(16):
        f = piece(j)
        first, second = first + pq[0, j] * f, second + pq[1, j] * f
    for h in range(2):
        own[3, h : h + 1, :] = jnp.sum(first[h], axis=0, keepdims=True)
        own[4, h : h + 1, :] = jnp.sum(second[h], axis=0, keepdims=True)

    for copy in halo_x:
        copy.wait_recv()
    ob, oal, obe, os1, os2, first_g, last_g = (own[k] for k in range(7))
    og = jnp.where(gx < NSEG - 1, joint(xs[1], xr[1]), 0.0)
    oal = oal + shunt_of(jnp.where(gx > 0, joint(xr[0], xs[0]), 0.0), first_g)
    obe = obe + shunt_of(last_g, og)
    r = 1.0 / (ob + obe + og)
    pa, pb = ob * r, og * r
    whole = (pa * og, oal + pa * obe, pb * obe, os1 + pa * os2, pb * os2)
    for k in range(5):
        mine[k] = whole[k]
    for k in range(2):
        pl.semaphore_wait(word_sem.at[k], 1)
    near_copies = [
        pltpu.make_async_remote_copy(
            src_ref=mine, dst_ref=near.at[k], send_sem=ns_sem.at[k], recv_sem=nr_sem.at[k],
            device_id=seg(-o), device_id_type=MESH,
        )
        for k, o in enumerate(NEAR)
    ]
    for k in (6, 5, 0, 4, 1, 3, 2):
        near_copies[k].start()

    steps = [(node, lo, hi, pa, pb, elim[k]) for k, (node, lo, hi, pa, pb, _) in enumerate(steps)]
    f = [piece(j) for j in range(16)]
    ends = {(j, j + 1): (f[j], None) for j in range(15)}
    inner = {}
    for node, lo, hi, pa, pb, r in steps:
        a, c = ends[lo, node], ends[node, hi]
        s = c[0] if a[1] is None else a[1] + c[0]
        inner[node] = s * r
        ends[lo, hi] = (a[0] + pa * s, pb * s if c[1] is None else c[1] + pb * s)
    s1, s2 = ends[0, 15]
    s2 = s2 + f[15]
    at_end = r15 * s2
    s1, s2 = jnp.where(last, s1, s1 + pa15 * s2), jnp.where(last, s2, pb15 * s2)
    middle = []
    for step, pa, pb, r in levels:
        bs1, bs2 = pltpu.roll(s1, 8 - step, 1), pltpu.roll(s2, 8 - step, 1)
        s = s2 + bs1
        middle.append(s * r)
        s1, s2 = s1 + pa * s, bs2 + pb * s
    for j, value in enumerate(descend(zero, zero, (middle, at_end, inner))):
        pq[2, j] = value

    for copy in near_copies:
        copy.wait_recv()
    item = {o: tuple(near[k, i] for i in range(5)) for k, o in enumerate(NEAR)}
    item[0] = whole
    ahead = combine(combine(item[1], item[2]), combine(item[3], item[4]))
    behind = combine(item[-3], item[-2])
    behind_own = combine(behind, combine(item[-1], item[0]))
    behind = combine(behind, item[-1])
    window = combine(behind_own, ahead)
    for k in range(5):
        mid[0, k] = ahead[k]
        mid[1, k] = window[k]
        mid[2, k] = behind_own[k]
    far_copies = [
        pltpu.make_async_remote_copy(
            src_ref=mid.at[0 if k == 0 else 2 if k == 7 else 1], dst_ref=far.at[k],
            send_sem=fs_sem.at[k], recv_sem=fr_sem.at[k],
            device_id=seg(-o), device_id_type=MESH,
        )
        for k, o in enumerate(FAR)
    ]
    for k in (3, 4, 2, 5, 1, 6, 0, 7):
        far_copies[k].start()
    for copy in far_copies:
        copy.wait_recv()
    chain = [ahead] + [tuple(far[k, i] for i in range(5)) for k in range(8)] + [behind]
    while len(chain) > 1:
        chain = [combine(*chain[k : k + 2]) if k + 1 < len(chain) else chain[k] for k in range(0, len(chain), 2)]
    _, right_g, left_g, right_s, left_s = chain[0]

    r = og / (og + right_g)
    end_g, end_s = obe + r * right_g, os2 + r * right_s
    r = 1.0 / (ob + end_g)
    start = (os1 + left_s + ob * r * end_s) / (oal + left_g + ob * r * end_g)
    end = r * (ob * start + end_s)
    start = jnp.stack([jnp.broadcast_to(start[h : h + 1, :], (8, 128)) for h in range(2)])
    end = jnp.stack([jnp.broadcast_to(end[h : h + 1, :], (8, 128)) for h in range(2)])
    for j in range(16):
        value = pq[2, j] + pq[0, j] * start + pq[1, j] * end
        for h in range(2):
            trans[h, pl.ds(j, 8, stride=16), :] = value[h]
    for h in range(2):
        out_ref[128 * h : 128 * h + 128, :] = trans[h].T

    for copy in halo + halo_x + near_copies + far_copies:
        copy.wait_send()


def local(thermal_field, material_state, beam_path_indicator, state_diffusivity_table):
    f32 = jnp.float32
    flat = (256, 128)
    hbm = pl.BlockSpec(memory_space=pltpu.HBM)
    dma = pltpu.SemaphoreType.DMA
    out = pl.pallas_call(
        kernel,
        out_shape=pltpu.VMEM(flat, f32),
        in_specs=[hbm, hbm, hbm, pl.BlockSpec(memory_space=pltpu.SMEM)],
        out_specs=pl.BlockSpec(memory_space=pltpu.VMEM),
        scratch_shapes=[
            pltpu.VMEM(flat, f32),
            pltpu.VMEM(flat, jnp.int32),
            pltpu.VMEM(flat, jnp.int32),
            pltpu.VMEM(flat, f32),
            pltpu.VMEM(flat, f32),
            pltpu.VMEM((2, 128, 128), f32),
            pltpu.VMEM((3, 16, 2, 8, 128), f32),
            pltpu.VMEM((14, 2, 8, 128), f32),
            pltpu.VMEM((2, 2, 8, 128), f32),
            pltpu.VMEM((2, 2, 8, 128), f32),
            pltpu.VMEM((2, 2, 128), f32),
            pltpu.VMEM((2, 2, 128), f32),
            pltpu.VMEM((7, 2, 128), f32),
            pltpu.VMEM((5, 2, 128), f32),
            pltpu.VMEM((len(NEAR), 5, 2, 128), f32),
            pltpu.VMEM((3, 5, 2, 128), f32),
            pltpu.VMEM((len(FAR), 5, 2, 128), f32),
            dma((3,)),
            dma((2,)),
            dma((2,)),
            dma((2,)),
            dma((2,)),
            dma((len(NEAR),)),
            dma((len(NEAR),)),
            dma((len(FAR),)),
            dma((len(FAR),)),
            pltpu.SemaphoreType.REGULAR((2,)),
        ],
        compiler_params=pltpu.CompilerParams(collective_id=0, has_side_effects=True),
        name="adi_x",
    )(
        thermal_field.reshape(flat),
        material_state.reshape(flat),
        beam_path_indicator.reshape(flat),
        state_diffusivity_table,
    )
    return out.reshape(thermal_field.shape)


def solution(mesh):
    in_specs = (P(None, "gy", "gx"), P(None, "gy", "gx"), P(None, "gy", "gx"), P())
    out_specs = P(None, "gy", "gx")
    return jax.shard_map(local, mesh=mesh, in_specs=in_specs, out_specs=out_specs, check_vma=False)
```

```python
import jax
import jax.numpy as jnp
from jax import lax
from jax.experimental import pallas as pl
from jax.experimental.pallas import tpu as pltpu
from jax.sharding import PartitionSpec as P

MESH = pl.DeviceIdType.MESH
RATIO = 65536.0
NSEG = 64
NGY = 8
NEAR = (-3, -2, -1, 1, 2, 3, 4)
GREET = (-2, -1, 1, 2, 16, 32, 48)
FAR = (4, 12, 20, 28, 36, 44, 52, 60)


def face(a, b):
    return 2.0 * a * b / (a + b)


def split(x):
    high = 4097.0 * x
    high = high - (high - x)
    return high, x - high


def exact_face(a, b):
    above, below = 2.0 * a * b, a + b
    q = above / below
    (qh, ql), (bh, bl) = split(q), split(below)
    p = q * below
    error = ((qh * bh - p) + qh * bl + ql * bh) + ql * bl
    return q + ((above - p) - error) / below


def shunt_of(left, right):
    once = 1.0 + left
    diag = once + right
    part = diag - once
    return (once - left) - ((once - (diag - part)) + (right - part))


def combine(a, b):
    ab, aal, abe, as1, as2 = a
    bb, bal, bbe, bs1, bs2 = b
    shunt = abe + bal
    r = 1.0 / (ab + bb + shunt)
    pa, pb = ab * r, bb * r
    s = as2 + bs1
    return (pa * bb, aal + pa * shunt, bbe + pb * shunt, as1 + pa * s, bs2 + pb * s)


def build(g, shunts, lo, hi):
    if hi - lo == 1:
        return (g[lo], shunts[lo], None), []
    half = 1
    while half * 2 < hi - lo:
        half *= 2
    mid = lo + half
    (ab, aal, abe), left = build(g, shunts, lo, mid)
    (bb, bal, bbe), right = build(g, shunts, mid, hi)
    shunt = bal if abe is None else bal + abe
    r = 1.0 / (ab + bb + shunt)
    pa, pb = ab * r, bb * r
    al = aal + pa * shunt
    be = pb * shunt if bbe is None else bbe + pb * shunt
    return (pa * bb, al, be), left + right + [(mid, lo, hi, pa, pb, r)]


def kernel(
    t_hbm, m_hbm, b_hbm, table_hbm, out_ref,
    table, tv, mv, bv, cv, fv, trans, pq, elim, hs, hr, xs, xr, own, mine, near, mid, far,
    load_sem, hs_sem, hr_sem, xs_sem, xr_sem, ns_sem, nr_sem, fs_sem, fr_sem, word_sem,
):
    gx, gy = lax.axis_index("gx"), lax.axis_index("gy")

    def seg(offset):
        return {"gx": lax.rem(gx + (offset % NSEG), NSEG)}

    def side(offset):
        return {"gy": lax.rem(gy + (offset % NGY), NGY)}

    barrier = pltpu.get_barrier_semaphore()
    greeted = [side(1), side(-1)] + [seg(o) for o in GREET]
    for device in greeted:
        pl.semaphore_signal(barrier, inc=1, device_id=device, device_id_type=MESH)

    loads = [
        pltpu.make_async_copy(src, dst, load_sem.at[k])
        for k, (src, dst) in enumerate(((table_hbm, table), (m_hbm, mv), (t_hbm, tv), (b_hbm, bv)))
    ]
    for load in loads:
        load.start()
    pl.semaphore_wait(barrier, len(greeted))
    for k in range(2):
        pl.semaphore_signal(word_sem.at[k], inc=1, device_id=seg(4 * k - 2), device_id_type=MESH)

    loads[0].wait()
    t0, t1, t2 = table[0], table[1], table[2]

    def conductivity(m):
        return jnp.where(m == 0, t0, jnp.where(m == 1, t1, t2))

    low, high = pl.ds(0, 8, stride=32), pl.ds(31, 8, stride=32)
    loads[1].wait()
    hs[0, 1] = conductivity(mv[low, :])
    hs[1, 1] = conductivity(mv[high, :])
    loads[2].wait()
    hs[0, 0] = tv[low, :]
    hs[1, 0] = tv[high, :]

    halo = [
        pltpu.make_async_remote_copy(
            src_ref=hs.at[k], dst_ref=hr.at[1 - k], send_sem=hs_sem.at[k], recv_sem=hr_sem.at[1 - k],
            device_id=side(2 * k - 1), device_id_type=MESH,
        )
        for k in range(2)
    ]
    for copy in halo:
        copy.start()

    cv[...] = conductivity(mv[...])
    for h in range(2):
        trans[h] = cv[128 * h : 128 * h + 128, :].T
        xs[0, h : h + 1, :] = trans[h, 0:1, :]
        xs[1, h : h + 1, :] = trans[h, 127:128, :]
    halo_x = [
        pltpu.make_async_remote_copy(
            src_ref=xs.at[k], dst_ref=xr.at[1 - k], send_sem=xs_sem.at[k], recv_sem=xr_sem.at[1 - k],
            device_id=seg(2 * k - 1), device_id_type=MESH,
        )
        for k in range(2)
    ]
    for copy in halo_x:
        copy.start()

    shape = (2, 8, 128)
    row = lax.broadcasted_iota(jnp.int32, shape, 1)

    tables = [jnp.full((8, 128), t, jnp.float32) for t in (t0, t1, t2)]
    faces = {}
    for i in range(3):
        for j in range(i, 3):
            faces[i, j] = faces[j, i] = RATIO * exact_face(tables[i], tables[j])[0:1, :]

    def joint(a, b):
        b0, b1 = b == t0, b == t1
        rows = [jnp.where(b0, faces[i, 0], jnp.where(b1, faces[i, 1], faces[i, 2])) for i in range(3)]
        return jnp.where(a == t0, rows[0], jnp.where(a == t1, rows[1], rows[2]))

    def piece(j):
        return jnp.stack([trans[h, pl.ds(j, 8, stride=16), :] for h in range(2)])

    cond = [piece(j) for j in range(16)]
    cond.append(pltpu.roll(cond[0], 7, 1))
    g = [joint(cond[j], cond[j + 1]) for j in range(16)]
    last = row == 7
    shunts = [jnp.where(row == 0, 0.0, shunt_of(pltpu.roll(g[15], 1, 1), g[0]))]
    shunts += [shunt_of(g[j - 1], g[j]) for j in range(1, 16)]
    (cb, cal, cbe), steps = build(g, shunts, 0, 15)
    cbe = cbe + jnp.where(last, 0.0, shunts[15])
    r15 = 1.0 / (cb + cbe + g[15])
    pa15, pb15 = cb * r15, g[15] * r15
    b = jnp.where(last, cb, pa15 * g[15])
    al = jnp.where(last, cal, cal + pa15 * cbe)
    be = jnp.where(last, cbe, pb15 * cbe)
    levels = []
    for step in (1, 2, 4):
        bb, bal, bbe = (pltpu.roll(v, 8 - step, 1) for v in (b, al, be))
        shunt = be + bal
        r = 1.0 / (b + bb + shunt)
        pa, pb = b * r, bb * r
        b, al, be = pa * bb, al + pa * shunt, bbe + pb * shunt
        levels.append((step, pa, pb, r))
    for h in range(2):
        own[0, h : h + 1, :] = b[h, 0:1, :]
        own[1, h : h + 1, :] = al[h, 0:1, :]
        own[2, h : h + 1, :] = be[h, 0:1, :]
        own[5, h : h + 1, :] = g[0][h, 0:1, :]
        own[6, h : h + 1, :] = g[14][h, 7:8, :]

    def spread(value, step):
        if step == 4:
            return jnp.broadcast_to(value[:, 0:1, :], shape)
        if step == 2:
            return jnp.where(row < 4, value[:, 0:1, :], value[:, 4:5, :])
        return jnp.where(row % 2 == 0, value, pltpu.roll(value, 1, 1))

    def descend(left, right, sources):
        for k, (step, pa, pb, _) in reversed(list(enumerate(levels))):
            centre = pa * left + pb * right
            if sources is not None:
                centre = centre + sources[0][k]
            centre = spread(centre, step)
            low = (row // step) % 2 == 0
            left, right = jnp.where(low, left, centre), jnp.where(low, centre, right)
        end = pa15 * left + pb15 * right
        if sources is not None:
            end = end + sources[1]
        values = {0: left, 15: jnp.where(last, right, end)}
        for node, lo, hi, pa, pb, _ in reversed(steps):
            values[node] = pa * values[lo] + pb * values[hi]
            if sources is not None:
                values[node] = values[node] + sources[2][node]
        return [values[j] for j in range(16)]

    one, zero = jnp.ones(shape, jnp.float32), jnp.zeros(shape, jnp.float32)
    for j, value in enumerate(descend(one, zero, None)):
        pq[0, j] = value
    for j, value in enumerate(descend(zero, one, None)):
        pq[1, j] = value
    for k, (_, _, _, _, _, r) in enumerate(steps):
        elim[k] = r

    loads[3].wait()
    line = lax.broadcasted_iota(jnp.int32, (32, 128), 0)
    below = None
    for z in range(8):
        here = slice(32 * z, 32 * z + 32)
        tz, cz = tv[here, :], cv[here, :]
        flux = jnp.where(line < 31, face(cz, pltpu.roll(cz, 31, 0)) * (pltpu.roll(tz, 31, 0) - tz), 0.0)
        value = tz + (flux - pltpu.roll(flux, 1, 0)) + 4.0 * bv[here, :].astype(jnp.float32)
        if below is not None:
            value = value - below
        if z < 7:
            above = slice(32 * z + 32, 32 * z + 64)
            below = face(cz, cv[above, :]) * (tv[above, :] - tz)
            value = value + below
        fv[here, :] = value

    for copy in halo:
        copy.wait_recv()
    flux = face(hs[1, 1], hr[1, 1]) * (hr[1, 0] - hs[1, 0])
    fv[high, :] = fv[high, :] + jnp.where(gy < NGY - 1, flux, 0.0)
    flux = face(hs[0, 1], hr[0, 1]) * (hs[0, 0] - hr[0, 0])
    fv[low, :] = fv[low, :] - jnp.where(gy > 0, flux, 0.0)
    for h in range(2):
        trans[h] = fv[128 * h : 128 * h + 128, :].T

    first, second = zero, zero
    for j in range(16):
        f = piece(j)
        first, second = first + pq[0, j] * f, second + pq[1, j] * f
    for h in range(2):
        own[3, h : h + 1, :] = jnp.sum(first[h], axis=0, keepdims=True)
        own[4, h : h + 1, :] = jnp.sum(second[h], axis=0, keepdims=True)

    for copy in halo_x:
        copy.wait_recv()
    ob, oal, obe, os1, os2, first_g, last_g = (own[k] for k in range(7))
    og = jnp.where(gx < NSEG - 1, joint(xs[1], xr[1]), 0.0)
    oal = oal + shunt_of(jnp.where(gx > 0, joint(xr[0], xs[0]), 0.0), first_g)
    obe = obe + shunt_of(last_g, og)
    r = 1.0 / (ob + obe + og)
    pa, pb = ob * r, og * r
    whole = (pa * og, oal + pa * obe, pb * obe, os1 + pa * os2, pb * os2)
    for k in range(5):
        mine[k] = whole[k]
    near_copies = [
        pltpu.make_async_remote_copy(
            src_ref=mine, dst_ref=near.at[k], send_sem=ns_sem.at[k], recv_sem=nr_sem.at[k],
            device_id=seg(-o), device_id_type=MESH,
        )
        for k, o in enumerate(NEAR)
    ]
    for k in (4, 2, 3):
        near_copies[k].start()
    for k in range(2):
        pl.semaphore_wait(word_sem.at[k], 1)
    for k in (6, 0, 5, 1):
        near_copies[k].start()

    steps = [(node, lo, hi, pa, pb, elim[k]) for k, (node, lo, hi, pa, pb, _) in enumerate(steps)]
    f = [piece(j) for j in range(16)]
    ends = {(j, j + 1): (f[j], None) for j in range(15)}
    inner = {}
    for node, lo, hi, pa, pb, r in steps:
        a, c = ends[lo, node], ends[node, hi]
        s = c[0] if a[1] is None else a[1] + c[0]
        inner[node] = s * r
        ends[lo, hi] = (a[0] + pa * s, pb * s if c[1] is None else c[1] + pb * s)
    s1, s2 = ends[0, 15]
    s2 = s2 + f[15]
    at_end = r15 * s2
    s1, s2 = jnp.where(last, s1, s1 + pa15 * s2), jnp.where(last, s2, pb15 * s2)
    middle = []
    for step, pa, pb, r in levels:
        bs1, bs2 = pltpu.roll(s1, 8 - step, 1), pltpu.roll(s2, 8 - step, 1)
        s = s2 + bs1
        middle.append(s * r)
        s1, s2 = s1 + pa * s, bs2 + pb * s
    for j, value in enumerate(descend(zero, zero, (middle, at_end, inner))):
        pq[2, j] = value

    for copy in near_copies:
        copy.wait_recv()
    item = {o: tuple(near[k, i] for i in range(5)) for k, o in enumerate(NEAR)}
    item[0] = whole
    ahead = combine(combine(item[1], item[2]), combine(item[3], item[4]))
    behind = combine(item[-3], item[-2])
    behind_own = combine(behind, combine(item[-1], item[0]))
    behind = combine(behind, item[-1])
    window = combine(behind_own, ahead)
    for k in range(5):
        mid[0, k] = ahead[k]
        mid[1, k] = window[k]
        mid[2, k] = behind_own[k]
    far_copies = [
        pltpu.make_async_remote_copy(
            src_ref=mid.at[0 if k == 0 else 2 if k == 7 else 1], dst_ref=far.at[k],
            send_sem=fs_sem.at[k], recv_sem=fr_sem.at[k],
            device_id=seg(-o), device_id_type=MESH,
        )
        for k, o in enumerate(FAR)
    ]
    for k in (3, 4, 2, 5, 1, 6, 0, 7):
        far_copies[k].start()
    for copy in far_copies:
        copy.wait_recv()
    chain = [ahead] + [tuple(far[k, i] for i in range(5)) for k in range(8)] + [behind]
    while len(chain) > 1:
        chain = [combine(*chain[k : k + 2]) if k + 1 < len(chain) else chain[k] for k in range(0, len(chain), 2)]
    _, right_g, left_g, right_s, left_s = chain[0]

    r = og / (og + right_g)
    end_g, end_s = obe + r * right_g, os2 + r * right_s
    r = 1.0 / (ob + end_g)
    start = (os1 + left_s + ob * r * end_s) / (oal + left_g + ob * r * end_g)
    end = r * (ob * start + end_s)
    start = jnp.stack([jnp.broadcast_to(start[h : h + 1, :], (8, 128)) for h in range(2)])
    end = jnp.stack([jnp.broadcast_to(end[h : h + 1, :], (8, 128)) for h in range(2)])
    for j in range(16):
        value = pq[2, j] + pq[0, j] * start + pq[1, j] * end
        for h in range(2):
            trans[h, pl.ds(j, 8, stride=16), :] = value[h]
    for h in range(2):
        out_ref[128 * h : 128 * h + 128, :] = trans[h].T

    for copy in halo + halo_x + near_copies + far_copies:
        copy.wait_send()


def local(thermal_field, material_state, beam_path_indicator, state_diffusivity_table):
    f32 = jnp.float32
    flat = (256, 128)
    hbm = pl.BlockSpec(memory_space=pltpu.HBM)
    dma = pltpu.SemaphoreType.DMA
    out = pl.pallas_call(
        kernel,
        out_shape=pltpu.VMEM(flat, f32),
        in_specs=[hbm] * 4,
        out_specs=pl.BlockSpec(memory_space=pltpu.VMEM),
        scratch_shapes=[
            pltpu.SMEM((3,), f32),
            pltpu.VMEM(flat, f32),
            pltpu.VMEM(flat, jnp.int32),
            pltpu.VMEM(flat, jnp.int32),
            pltpu.VMEM(flat, f32),
            pltpu.VMEM(flat, f32),
            pltpu.VMEM((2, 128, 128), f32),
            pltpu.VMEM((3, 16, 2, 8, 128), f32),
            pltpu.VMEM((14, 2, 8, 128), f32),
            pltpu.VMEM((2, 2, 8, 128), f32),
            pltpu.VMEM((2, 2, 8, 128), f32),
            pltpu.VMEM((2, 2, 128), f32),
            pltpu.VMEM((2, 2, 128), f32),
            pltpu.VMEM((7, 2, 128), f32),
            pltpu.VMEM((5, 2, 128), f32),
            pltpu.VMEM((len(NEAR), 5, 2, 128), f32),
            pltpu.VMEM((3, 5, 2, 128), f32),
            pltpu.VMEM((len(FAR), 5, 2, 128), f32),
            dma((4,)),
            dma((2,)),
            dma((2,)),
            dma((2,)),
            dma((2,)),
            dma((len(NEAR),)),
            dma((len(NEAR),)),
            dma((len(FAR),)),
            dma((len(FAR),)),
            pltpu.SemaphoreType.REGULAR((2,)),
        ],
        compiler_params=pltpu.CompilerParams(collective_id=0, has_side_effects=True),
        name="adi_x",
    )(
        thermal_field.reshape(flat),
        material_state.reshape(flat),
        beam_path_indicator.reshape(flat),
        state_diffusivity_table,
    )
    return out.reshape(thermal_field.shape)


def solution(mesh):
    in_specs = (P(None, "gy", "gx"), P(None, "gy", "gx"), P(None, "gy", "gx"), P())
    out_specs = P(None, "gy", "gx")
    return jax.shard_map(local, mesh=mesh, in_specs=in_specs, out_specs=out_specs, check_vma=False)
```

```python
import jax
import jax.numpy as jnp
from jax import lax
from jax.experimental import pallas as pl
from jax.experimental.pallas import tpu as pltpu
from jax.sharding import PartitionSpec as P

MESH = pl.DeviceIdType.MESH
RATIO = 65536.0
NSEG = 64
NGY = 8
NEAR = (-4, -3, -2, -1, 1, 2, 3)
GREET = (-2, -1, 1, 2, 16, 32, 48)
FAR = (4, 12, 20, 28, 36, 44, 52, 60)


def face(a, b):
    return 2.0 * a * b / (a + b)


def split(x):
    high = 4097.0 * x
    high = high - (high - x)
    return high, x - high


def exact_face(a, b):
    above, below = 2.0 * a * b, a + b
    q = above / below
    (qh, ql), (bh, bl) = split(q), split(below)
    p = q * below
    error = ((qh * bh - p) + qh * bl + ql * bh) + ql * bl
    return q + ((above - p) - error) / below


def shunt_of(left, right):
    once = 1.0 + left
    diag = once + right
    part = diag - once
    return (once - left) - ((once - (diag - part)) + (right - part))


def combine(a, b):
    ab, aal, abe, as1, as2 = a
    bb, bal, bbe, bs1, bs2 = b
    shunt = abe + bal
    r = 1.0 / (ab + bb + shunt)
    pa, pb = ab * r, bb * r
    s = as2 + bs1
    return (pa * bb, aal + pa * shunt, bbe + pb * shunt, as1 + pa * s, bs2 + pb * s)


def build(g, shunts, lo, hi):
    if hi - lo == 1:
        return (g[lo], shunts[lo], None), []
    half = 1
    while half * 2 < hi - lo:
        half *= 2
    mid = lo + half
    (ab, aal, abe), left = build(g, shunts, lo, mid)
    (bb, bal, bbe), right = build(g, shunts, mid, hi)
    shunt = bal if abe is None else bal + abe
    r = 1.0 / (ab + bb + shunt)
    pa, pb = ab * r, bb * r
    al = aal + pa * shunt
    be = pb * shunt if bbe is None else bbe + pb * shunt
    return (pa * bb, al, be), left + right + [(mid, lo, hi, pa, pb, r)]


def kernel(
    t_hbm, m_hbm, b_hbm, table_hbm, out_ref,
    table, tv, mv, bv, cv, fv, trans, pq, elim, hs, hr, xs, xr, own, mine, near, mid, far,
    load_sem, hs_sem, hr_sem, xs_sem, xr_sem, ns_sem, nr_sem, fs_sem, fr_sem, word_sem,
):
    gx, gy = lax.axis_index("gx"), lax.axis_index("gy")

    def seg(offset):
        return {"gx": lax.rem(gx + (offset % NSEG), NSEG)}

    def side(offset):
        return {"gy": lax.rem(gy + (offset % NGY), NGY)}

    barrier = pltpu.get_barrier_semaphore()
    greeted = [side(1), side(-1)] + [seg(o) for o in GREET]
    for device in greeted:
        pl.semaphore_signal(barrier, inc=1, device_id=device, device_id_type=MESH)

    loads = [
        pltpu.make_async_copy(src, dst, load_sem.at[k])
        for k, (src, dst) in enumerate(((table_hbm, table), (m_hbm, mv), (t_hbm, tv), (b_hbm, bv)))
    ]
    for load in loads:
        load.start()
    loads[0].wait()
    t0, t1, t2 = table[0], table[1], table[2]

    def conductivity(m):
        return jnp.where(m == 0, t0, jnp.where(m == 1, t1, t2))

    low, high = pl.ds(0, 8, stride=32), pl.ds(31, 8, stride=32)
    loads[1].wait()
    hs[0, 1] = conductivity(mv[low, :])
    hs[1, 1] = conductivity(mv[high, :])
    loads[2].wait()
    hs[0, 0] = tv[low, :]
    hs[1, 0] = tv[high, :]

    cv[...] = conductivity(mv[...])
    for h in range(2):
        trans[h] = cv[128 * h : 128 * h + 128, :].T
        xs[0, h : h + 1, :] = trans[h, 0:1, :]
        xs[1, h : h + 1, :] = trans[h, 127:128, :]
    pl.semaphore_wait(barrier, len(greeted))
    for k in range(2):
        pl.semaphore_signal(word_sem.at[k], inc=1, device_id=seg(4 * k - 2), device_id_type=MESH)

    halo = [
        pltpu.make_async_remote_copy(
            src_ref=hs.at[k], dst_ref=hr.at[1 - k], send_sem=hs_sem.at[k], recv_sem=hr_sem.at[1 - k],
            device_id=side(2 * k - 1), device_id_type=MESH,
        )
        for k in range(2)
    ]
    for copy in halo:
        copy.start()

    halo_x = [
        pltpu.make_async_remote_copy(
            src_ref=xs.at[k], dst_ref=xr.at[1 - k], send_sem=xs_sem.at[k], recv_sem=xr_sem.at[1 - k],
            device_id=seg(2 * k - 1), device_id_type=MESH,
        )
        for k in range(2)
    ]
    for copy in halo_x:
        copy.start()

    shape = (2, 8, 128)
    row = lax.broadcasted_iota(jnp.int32, shape, 1)

    tables = [jnp.full((8, 128), t, jnp.float32) for t in (t0, t1, t2)]
    faces = {}
    for i in range(3):
        for j in range(i, 3):
            faces[i, j] = faces[j, i] = RATIO * exact_face(tables[i], tables[j])[0:1, :]

    def joint(a, b):
        b0, b1 = b == t0, b == t1
        rows = [jnp.where(b0, faces[i, 0], jnp.where(b1, faces[i, 1], faces[i, 2])) for i in range(3)]
        return jnp.where(a == t0, rows[0], jnp.where(a == t1, rows[1], rows[2]))

    def piece(j):
        return jnp.stack([trans[h, pl.ds(j, 8, stride=16), :] for h in range(2)])

    cond = [piece(j) for j in range(16)]
    cond.append(pltpu.roll(cond[0], 7, 1))
    g = [joint(cond[j], cond[j + 1]) for j in range(16)]
    last = row == 7
    shunts = [jnp.where(row == 0, 0.0, shunt_of(pltpu.roll(g[15], 1, 1), g[0]))]
    shunts += [shunt_of(g[j - 1], g[j]) for j in range(1, 16)]
    (cb, cal, cbe), steps = build(g, shunts, 0, 15)
    cbe = cbe + jnp.where(last, 0.0, shunts[15])
    r15 = 1.0 / (cb + cbe + g[15])
    pa15, pb15 = cb * r15, g[15] * r15
    b = jnp.where(last, cb, pa15 * g[15])
    al = jnp.where(last, cal, cal + pa15 * cbe)
    be = jnp.where(last, cbe, pb15 * cbe)
    levels = []
    for step in (1, 2, 4):
        bb, bal, bbe = (pltpu.roll(v, 8 - step, 1) for v in (b, al, be))
        shunt = be + bal
        r = 1.0 / (b + bb + shunt)
        pa, pb = b * r, bb * r
        b, al, be = pa * bb, al + pa * shunt, bbe + pb * shunt
        levels.append((step, pa, pb, r))
    for h in range(2):
        own[0, h : h + 1, :] = b[h, 0:1, :]
        own[1, h : h + 1, :] = al[h, 0:1, :]
        own[2, h : h + 1, :] = be[h, 0:1, :]
        own[5, h : h + 1, :] = g[0][h, 0:1, :]
        own[6, h : h + 1, :] = g[14][h, 7:8, :]

    def spread(value, step):
        if step == 4:
            return jnp.broadcast_to(value[:, 0:1, :], shape)
        if step == 2:
            return jnp.where(row < 4, value[:, 0:1, :], value[:, 4:5, :])
        return jnp.where(row % 2 == 0, value, pltpu.roll(value, 1, 1))

    def descend(left, right, sources):
        for k, (step, pa, pb, _) in reversed(list(enumerate(levels))):
            centre = pa * left + pb * right
            if sources is not None:
                centre = centre + sources[0][k]
            centre = spread(centre, step)
            low = (row // step) % 2 == 0
            left, right = jnp.where(low, left, centre), jnp.where(low, centre, right)
        end = pa15 * left + pb15 * right
        if sources is not None:
            end = end + sources[1]
        values = {0: left, 15: jnp.where(last, right, end)}
        for node, lo, hi, pa, pb, _ in reversed(steps):
            values[node] = pa * values[lo] + pb * values[hi]
            if sources is not None:
                values[node] = values[node] + sources[2][node]
        return [values[j] for j in range(16)]

    one, zero = jnp.ones(shape, jnp.float32), jnp.zeros(shape, jnp.float32)
    for j, value in enumerate(descend(one, zero, None)):
        pq[0, j] = value
    for j, value in enumerate(descend(zero, one, None)):
        pq[1, j] = value
    for k, (_, _, _, _, _, r) in enumerate(steps):
        elim[k] = r

    loads[3].wait()
    line = lax.broadcasted_iota(jnp.int32, (32, 128), 0)
    below = None
    for z in range(8):
        here = slice(32 * z, 32 * z + 32)
        tz, cz = tv[here, :], cv[here, :]
        flux = jnp.where(line < 31, face(cz, pltpu.roll(cz, 31, 0)) * (pltpu.roll(tz, 31, 0) - tz), 0.0)
        value = tz + (flux - pltpu.roll(flux, 1, 0)) + 4.0 * bv[here, :].astype(jnp.float32)
        if below is not None:
            value = value - below
        if z < 7:
            above = slice(32 * z + 32, 32 * z + 64)
            below = face(cz, cv[above, :]) * (tv[above, :] - tz)
            value = value + below
        fv[here, :] = value

    for copy in halo:
        copy.wait_recv()
    flux = face(hs[1, 1], hr[1, 1]) * (hr[1, 0] - hs[1, 0])
    fv[high, :] = fv[high, :] + jnp.where(gy < NGY - 1, flux, 0.0)
    flux = face(hs[0, 1], hr[0, 1]) * (hs[0, 0] - hr[0, 0])
    fv[low, :] = fv[low, :] - jnp.where(gy > 0, flux, 0.0)
    for h in range(2):
        trans[h] = fv[128 * h : 128 * h + 128, :].T

    first, second = zero, zero
    for j in range(16):
        f = piece(j)
        first, second = first + pq[0, j] * f, second + pq[1, j] * f
    for h in range(2):
        own[3, h : h + 1, :] = jnp.sum(first[h], axis=0, keepdims=True)
        own[4, h : h + 1, :] = jnp.sum(second[h], axis=0, keepdims=True)

    for copy in halo_x:
        copy.wait_recv()
    ob, oal, obe, os1, os2, first_g, last_g = (own[k] for k in range(7))
    og = jnp.where(gx < NSEG - 1, joint(xs[1], xr[1]), 0.0)
    oal = oal + shunt_of(jnp.where(gx > 0, joint(xr[0], xs[0]), 0.0), first_g)
    obe = obe + shunt_of(last_g, og)
    r = 1.0 / (ob + obe + og)
    pa, pb = ob * r, og * r
    whole = (pa * og, oal + pa * obe, pb * obe, os1 + pa * os2, pb * os2)
    for k in range(5):
        mine[k] = whole[k]
    near_copies = [
        pltpu.make_async_remote_copy(
            src_ref=mine, dst_ref=near.at[k], send_sem=ns_sem.at[k], recv_sem=nr_sem.at[k],
            device_id=seg(-o), device_id_type=MESH,
        )
        for k, o in enumerate(NEAR)
    ]
    for k in (2, 3, 4):
        near_copies[k].start()
    for k in range(2):
        pl.semaphore_wait(word_sem.at[k], 1)
    for k in (0, 1, 6, 5):
        near_copies[k].start()

    steps = [(node, lo, hi, pa, pb, elim[k]) for k, (node, lo, hi, pa, pb, _) in enumerate(steps)]
    f = [piece(j) for j in range(16)]
    ends = {(j, j + 1): (f[j], None) for j in range(15)}
    inner = {}
    for node, lo, hi, pa, pb, r in steps:
        a, c = ends[lo, node], ends[node, hi]
        s = c[0] if a[1] is None else a[1] + c[0]
        inner[node] = s * r
        ends[lo, hi] = (a[0] + pa * s, pb * s if c[1] is None else c[1] + pb * s)
    s1, s2 = ends[0, 15]
    s2 = s2 + f[15]
    at_end = r15 * s2
    s1, s2 = jnp.where(last, s1, s1 + pa15 * s2), jnp.where(last, s2, pb15 * s2)
    middle = []
    for step, pa, pb, r in levels:
        bs1, bs2 = pltpu.roll(s1, 8 - step, 1), pltpu.roll(s2, 8 - step, 1)
        s = s2 + bs1
        middle.append(s * r)
        s1, s2 = s1 + pa * s, bs2 + pb * s
    for j, value in enumerate(descend(zero, zero, (middle, at_end, inner))):
        pq[2, j] = value

    for copy in near_copies:
        copy.wait_recv()
    item = {o: tuple(near[k, i] for i in range(5)) for k, o in enumerate(NEAR)}
    item[0] = whole
    behind = combine(combine(item[-4], item[-3]), combine(item[-2], item[-1]))
    ahead = combine(item[2], item[3])
    own_ahead = combine(combine(item[0], item[1]), ahead)
    ahead = combine(item[1], ahead)
    window = combine(behind, own_ahead)
    for k in range(5):
        mid[0, k] = own_ahead[k]
        mid[1, k] = window[k]
        mid[2, k] = behind[k]
    far_copies = [
        pltpu.make_async_remote_copy(
            src_ref=mid.at[0 if k == 0 else 2 if k == 7 else 1], dst_ref=far.at[k],
            send_sem=fs_sem.at[k], recv_sem=fr_sem.at[k],
            device_id=seg(-o), device_id_type=MESH,
        )
        for k, o in enumerate(FAR)
    ]
    for k in (3, 4, 2, 5, 1, 6, 0, 7):
        far_copies[k].start()
    for copy in far_copies:
        copy.wait_recv()
    chain = [ahead] + [tuple(far[k, i] for i in range(5)) for k in range(8)] + [behind]
    while len(chain) > 1:
        chain = [combine(*chain[k : k + 2]) if k + 1 < len(chain) else chain[k] for k in range(0, len(chain), 2)]
    _, right_g, left_g, right_s, left_s = chain[0]

    r = og / (og + right_g)
    end_g, end_s = obe + r * right_g, os2 + r * right_s
    r = 1.0 / (ob + end_g)
    start = (os1 + left_s + ob * r * end_s) / (oal + left_g + ob * r * end_g)
    end = r * (ob * start + end_s)
    start = jnp.stack([jnp.broadcast_to(start[h : h + 1, :], (8, 128)) for h in range(2)])
    end = jnp.stack([jnp.broadcast_to(end[h : h + 1, :], (8, 128)) for h in range(2)])
    for j in range(16):
        value = pq[2, j] + pq[0, j] * start + pq[1, j] * end
        for h in range(2):
            trans[h, pl.ds(j, 8, stride=16), :] = value[h]
    for h in range(2):
        out_ref[128 * h : 128 * h + 128, :] = trans[h].T

    for copy in halo + halo_x + near_copies + far_copies:
        copy.wait_send()


def local(thermal_field, material_state, beam_path_indicator, state_diffusivity_table):
    f32 = jnp.float32
    flat = (256, 128)
    hbm = pl.BlockSpec(memory_space=pltpu.HBM)
    dma = pltpu.SemaphoreType.DMA
    out = pl.pallas_call(
        kernel,
        out_shape=pltpu.VMEM(flat, f32),
        in_specs=[hbm] * 4,
        out_specs=pl.BlockSpec(memory_space=pltpu.VMEM),
        scratch_shapes=[
            pltpu.SMEM((3,), f32),
            pltpu.VMEM(flat, f32),
            pltpu.VMEM(flat, jnp.int32),
            pltpu.VMEM(flat, jnp.int32),
            pltpu.VMEM(flat, f32),
            pltpu.VMEM(flat, f32),
            pltpu.VMEM((2, 128, 128), f32),
            pltpu.VMEM((3, 16, 2, 8, 128), f32),
            pltpu.VMEM((14, 2, 8, 128), f32),
            pltpu.VMEM((2, 2, 8, 128), f32),
            pltpu.VMEM((2, 2, 8, 128), f32),
            pltpu.VMEM((2, 2, 128), f32),
            pltpu.VMEM((2, 2, 128), f32),
            pltpu.VMEM((7, 2, 128), f32),
            pltpu.VMEM((5, 2, 128), f32),
            pltpu.VMEM((len(NEAR), 5, 2, 128), f32),
            pltpu.VMEM((3, 5, 2, 128), f32),
            pltpu.VMEM((len(FAR), 5, 2, 128), f32),
            dma((4,)),
            dma((2,)),
            dma((2,)),
            dma((2,)),
            dma((2,)),
            dma((len(NEAR),)),
            dma((len(NEAR),)),
            dma((len(FAR),)),
            dma((len(FAR),)),
            pltpu.SemaphoreType.REGULAR((2,)),
        ],
        compiler_params=pltpu.CompilerParams(collective_id=0, has_side_effects=True),
        name="adi_x",
    )(
        thermal_field.reshape(flat),
        material_state.reshape(flat),
        beam_path_indicator.reshape(flat),
        state_diffusivity_table,
    )
    return out.reshape(thermal_field.shape)


def solution(mesh):
    in_specs = (P(None, "gy", "gx"), P(None, "gy", "gx"), P(None, "gy", "gx"), P())
    out_specs = P(None, "gy", "gx")
    return jax.shard_map(local, mesh=mesh, in_specs=in_specs, out_specs=out_specs, check_vma=False)
```

```python
import jax
import jax.numpy as jnp
from jax import lax
from jax.experimental import pallas as pl
from jax.experimental.pallas import tpu as pltpu
from jax.sharding import PartitionSpec as P

MESH = pl.DeviceIdType.MESH
RATIO = 65536.0
NSEG = 64
NGY = 8
NEAR = (-4, -3, -2, -1, 1, 2, 3)
GREET = (-3, -2, -1, 1, 2, 16, 32, 48)
FAR = (4, 12, 20, 28, 36, 44, 52, 60)


def face(a, b):
    return 2.0 * a * b / (a + b)


def split(x):
    high = 4097.0 * x
    high = high - (high - x)
    return high, x - high


def exact_face(a, b):
    above, below = 2.0 * a * b, a + b
    q = above / below
    (qh, ql), (bh, bl) = split(q), split(below)
    p = q * below
    error = ((qh * bh - p) + qh * bl + ql * bh) + ql * bl
    return q + ((above - p) - error) / below


def shunt_of(left, right):
    once = 1.0 + left
    diag = once + right
    part = diag - once
    return (once - left) - ((once - (diag - part)) + (right - part))


def combine(a, b):
    ab, aal, abe, as1, as2 = a
    bb, bal, bbe, bs1, bs2 = b
    shunt = abe + bal
    r = 1.0 / (ab + bb + shunt)
    pa, pb = ab * r, bb * r
    s = as2 + bs1
    return (pa * bb, aal + pa * shunt, bbe + pb * shunt, as1 + pa * s, bs2 + pb * s)


def build(g, shunts, lo, hi):
    if hi - lo == 1:
        return (g[lo], shunts[lo], None), []
    half = 1
    while half * 2 < hi - lo:
        half *= 2
    mid = lo + half
    (ab, aal, abe), left = build(g, shunts, lo, mid)
    (bb, bal, bbe), right = build(g, shunts, mid, hi)
    shunt = bal if abe is None else bal + abe
    r = 1.0 / (ab + bb + shunt)
    pa, pb = ab * r, bb * r
    al = aal + pa * shunt
    be = pb * shunt if bbe is None else bbe + pb * shunt
    return (pa * bb, al, be), left + right + [(mid, lo, hi, pa, pb, r)]


def kernel(
    t_hbm, m_hbm, b_hbm, table_hbm, out_ref,
    table, tv, mv, bv, cv, fv, trans, pq, elim, hs, hr, xs, xr, own, mine, near, mid, far,
    load_sem, hs_sem, hr_sem, xs_sem, xr_sem, ns_sem, nr_sem, fs_sem, fr_sem,
):
    gx, gy = lax.axis_index("gx"), lax.axis_index("gy")

    def seg(offset):
        return {"gx": lax.rem(gx + (offset % NSEG), NSEG)}

    def side(offset):
        return {"gy": lax.rem(gy + (offset % NGY), NGY)}

    barrier = pltpu.get_barrier_semaphore()
    greeted = [side(1), side(-1)] + [seg(o) for o in GREET]
    for device in greeted:
        pl.semaphore_signal(barrier, inc=1, device_id=device, device_id_type=MESH)

    loads = [
        pltpu.make_async_copy(src, dst, load_sem.at[k])
        for k, (src, dst) in enumerate(((table_hbm, table), (m_hbm, mv), (t_hbm, tv), (b_hbm, bv)))
    ]
    for load in loads:
        load.start()
    loads[0].wait()
    t0, t1, t2 = table[0], table[1], table[2]

    def conductivity(m):
        return jnp.where(m == 0, t0, jnp.where(m == 1, t1, t2))

    low, high = pl.ds(0, 8, stride=32), pl.ds(31, 8, stride=32)
    loads[1].wait()
    hs[0, 1] = conductivity(mv[low, :])
    hs[1, 1] = conductivity(mv[high, :])
    loads[2].wait()
    hs[0, 0] = tv[low, :]
    hs[1, 0] = tv[high, :]

    pl.semaphore_wait(barrier, len(greeted))
    halo = [
        pltpu.make_async_remote_copy(
            src_ref=hs.at[k], dst_ref=hr.at[1 - k], send_sem=hs_sem.at[k], recv_sem=hr_sem.at[1 - k],
            device_id=side(2 * k - 1), device_id_type=MESH,
        )
        for k in range(2)
    ]
    for copy in halo:
        copy.start()
    cv[...] = conductivity(mv[...])
    for h in range(2):
        trans[h] = cv[128 * h : 128 * h + 128, :].T
        xs[0, h : h + 1, :] = trans[h, 0:1, :]
        xs[1, h : h + 1, :] = trans[h, 127:128, :]

    halo_x = [
        pltpu.make_async_remote_copy(
            src_ref=xs.at[k], dst_ref=xr.at[1 - k], send_sem=xs_sem.at[k], recv_sem=xr_sem.at[1 - k],
            device_id=seg(2 * k - 1), device_id_type=MESH,
        )
        for k in range(2)
    ]
    for copy in halo_x:
        copy.start()

    shape = (2, 8, 128)
    row = lax.broadcasted_iota(jnp.int32, shape, 1)

    tables = [jnp.full((8, 128), t, jnp.float32) for t in (t0, t1, t2)]
    faces = {}
    for i in range(3):
        for j in range(i, 3):
            faces[i, j] = faces[j, i] = RATIO * exact_face(tables[i], tables[j])[0:1, :]

    def joint(a, b):
        b0, b1 = b == t0, b == t1
        rows = [jnp.where(b0, faces[i, 0], jnp.where(b1, faces[i, 1], faces[i, 2])) for i in range(3)]
        return jnp.where(a == t0, rows[0], jnp.where(a == t1, rows[1], rows[2]))

    def piece(j):
        return jnp.stack([trans[h, pl.ds(j, 8, stride=16), :] for h in range(2)])

    cond = [piece(j) for j in range(16)]
    cond.append(pltpu.roll(cond[0], 7, 1))
    g = [joint(cond[j], cond[j + 1]) for j in range(16)]
    last = row == 7
    shunts = [jnp.where(row == 0, 0.0, shunt_of(pltpu.roll(g[15], 1, 1), g[0]))]
    shunts += [shunt_of(g[j - 1], g[j]) for j in range(1, 16)]
    (cb, cal, cbe), steps = build(g, shunts, 0, 15)
    cbe = cbe + jnp.where(last, 0.0, shunts[15])
    r15 = 1.0 / (cb + cbe + g[15])
    pa15, pb15 = cb * r15, g[15] * r15
    b = jnp.where(last, cb, pa15 * g[15])
    al = jnp.where(last, cal, cal + pa15 * cbe)
    be = jnp.where(last, cbe, pb15 * cbe)
    levels = []
    for step in (1, 2, 4):
        bb, bal, bbe = (pltpu.roll(v, 8 - step, 1) for v in (b, al, be))
        shunt = be + bal
        r = 1.0 / (b + bb + shunt)
        pa, pb = b * r, bb * r
        b, al, be = pa * bb, al + pa * shunt, bbe + pb * shunt
        levels.append((step, pa, pb, r))
    for h in range(2):
        own[0, h : h + 1, :] = b[h, 0:1, :]
        own[1, h : h + 1, :] = al[h, 0:1, :]
        own[2, h : h + 1, :] = be[h, 0:1, :]
        own[5, h : h + 1, :] = g[0][h, 0:1, :]
        own[6, h : h + 1, :] = g[14][h, 7:8, :]

    def spread(value, step):
        if step == 4:
            return jnp.broadcast_to(value[:, 0:1, :], shape)
        if step == 2:
            return jnp.where(row < 4, value[:, 0:1, :], value[:, 4:5, :])
        return jnp.where(row % 2 == 0, value, pltpu.roll(value, 1, 1))

    def descend(left, right, sources):
        for k, (step, pa, pb, _) in reversed(list(enumerate(levels))):
            centre = pa * left + pb * right
            if sources is not None:
                centre = centre + sources[0][k]
            centre = spread(centre, step)
            low = (row // step) % 2 == 0
            left, right = jnp.where(low, left, centre), jnp.where(low, centre, right)
        end = pa15 * left + pb15 * right
        if sources is not None:
            end = end + sources[1]
        values = {0: left, 15: jnp.where(last, right, end)}
        for node, lo, hi, pa, pb, _ in reversed(steps):
            values[node] = pa * values[lo] + pb * values[hi]
            if sources is not None:
                values[node] = values[node] + sources[2][node]
        return [values[j] for j in range(16)]

    one, zero = jnp.ones(shape, jnp.float32), jnp.zeros(shape, jnp.float32)
    for j, value in enumerate(descend(one, zero, None)):
        pq[0, j] = value
    for j, value in enumerate(descend(zero, one, None)):
        pq[1, j] = value
    for k, (_, _, _, _, _, r) in enumerate(steps):
        elim[k] = r

    loads[3].wait()
    line = lax.broadcasted_iota(jnp.int32, (32, 128), 0)
    below = None
    for z in range(8):
        here = slice(32 * z, 32 * z + 32)
        tz, cz = tv[here, :], cv[here, :]
        flux = jnp.where(line < 31, face(cz, pltpu.roll(cz, 31, 0)) * (pltpu.roll(tz, 31, 0) - tz), 0.0)
        value = tz + (flux - pltpu.roll(flux, 1, 0)) + 4.0 * bv[here, :].astype(jnp.float32)
        if below is not None:
            value = value - below
        if z < 7:
            above = slice(32 * z + 32, 32 * z + 64)
            below = face(cz, cv[above, :]) * (tv[above, :] - tz)
            value = value + below
        fv[here, :] = value

    for copy in halo:
        copy.wait_recv()
    flux = face(hs[1, 1], hr[1, 1]) * (hr[1, 0] - hs[1, 0])
    fv[high, :] = fv[high, :] + jnp.where(gy < NGY - 1, flux, 0.0)
    flux = face(hs[0, 1], hr[0, 1]) * (hs[0, 0] - hr[0, 0])
    fv[low, :] = fv[low, :] - jnp.where(gy > 0, flux, 0.0)
    for h in range(2):
        trans[h] = fv[128 * h : 128 * h + 128, :].T

    first, second = zero, zero
    for j in range(16):
        f = piece(j)
        first, second = first + pq[0, j] * f, second + pq[1, j] * f
    for h in range(2):
        own[3, h : h + 1, :] = jnp.sum(first[h], axis=0, keepdims=True)
        own[4, h : h + 1, :] = jnp.sum(second[h], axis=0, keepdims=True)

    for copy in halo_x:
        copy.wait_recv()
    ob, oal, obe, os1, os2, first_g, last_g = (own[k] for k in range(7))
    og = jnp.where(gx < NSEG - 1, joint(xs[1], xr[1]), 0.0)
    oal = oal + shunt_of(jnp.where(gx > 0, joint(xr[0], xs[0]), 0.0), first_g)
    obe = obe + shunt_of(last_g, og)
    r = 1.0 / (ob + obe + og)
    pa, pb = ob * r, og * r
    whole = (pa * og, oal + pa * obe, pb * obe, os1 + pa * os2, pb * os2)
    for k in range(5):
        mine[k] = whole[k]
    near_copies = [
        pltpu.make_async_remote_copy(
            src_ref=mine, dst_ref=near.at[k], send_sem=ns_sem.at[k], recv_sem=nr_sem.at[k],
            device_id=seg(-o), device_id_type=MESH,
        )
        for k, o in enumerate(NEAR)
    ]
    for k in (0, 1, 6, 2, 5, 3, 4):
        near_copies[k].start()

    steps = [(node, lo, hi, pa, pb, elim[k]) for k, (node, lo, hi, pa, pb, _) in enumerate(steps)]
    f = [piece(j) for j in range(16)]
    ends = {(j, j + 1): (f[j], None) for j in range(15)}
    inner = {}
    for node, lo, hi, pa, pb, r in steps:
        a, c = ends[lo, node], ends[node, hi]
        s = c[0] if a[1] is None else a[1] + c[0]
        inner[node] = s * r
        ends[lo, hi] = (a[0] + pa * s, pb * s if c[1] is None else c[1] + pb * s)
    s1, s2 = ends[0, 15]
    s2 = s2 + f[15]
    at_end = r15 * s2
    s1, s2 = jnp.where(last, s1, s1 + pa15 * s2), jnp.where(last, s2, pb15 * s2)
    middle = []
    for step, pa, pb, r in levels:
        bs1, bs2 = pltpu.roll(s1, 8 - step, 1), pltpu.roll(s2, 8 - step, 1)
        s = s2 + bs1
        middle.append(s * r)
        s1, s2 = s1 + pa * s, bs2 + pb * s
    for j, value in enumerate(descend(zero, zero, (middle, at_end, inner))):
        pq[2, j] = value

    for copy in near_copies:
        copy.wait_recv()
    item = {o: tuple(near[k, i] for i in range(5)) for k, o in enumerate(NEAR)}
    item[0] = whole
    behind = combine(combine(item[-4], item[-3]), combine(item[-2], item[-1]))
    ahead = combine(item[2], item[3])
    own_ahead = combine(combine(item[0], item[1]), ahead)
    ahead = combine(item[1], ahead)
    window = combine(behind, own_ahead)
    for k in range(5):
        mid[0, k] = own_ahead[k]
        mid[1, k] = window[k]
        mid[2, k] = behind[k]
    far_copies = [
        pltpu.make_async_remote_copy(
            src_ref=mid.at[0 if k == 0 else 2 if k == 7 else 1], dst_ref=far.at[k],
            send_sem=fs_sem.at[k], recv_sem=fr_sem.at[k],
            device_id=seg(-o), device_id_type=MESH,
        )
        for k, o in enumerate(FAR)
    ]
    for k in (3, 4, 2, 5, 1, 6, 0, 7):
        far_copies[k].start()
    for copy in far_copies:
        copy.wait_recv()
    chain = [ahead] + [tuple(far[k, i] for i in range(5)) for k in range(8)] + [behind]
    while len(chain) > 1:
        chain = [combine(*chain[k : k + 2]) if k + 1 < len(chain) else chain[k] for k in range(0, len(chain), 2)]
    _, right_g, left_g, right_s, left_s = chain[0]

    r = og / (og + right_g)
    end_g, end_s = obe + r * right_g, os2 + r * right_s
    r = 1.0 / (ob + end_g)
    start = (os1 + left_s + ob * r * end_s) / (oal + left_g + ob * r * end_g)
    end = r * (ob * start + end_s)
    start = jnp.stack([jnp.broadcast_to(start[h : h + 1, :], (8, 128)) for h in range(2)])
    end = jnp.stack([jnp.broadcast_to(end[h : h + 1, :], (8, 128)) for h in range(2)])
    for j in range(16):
        value = pq[2, j] + pq[0, j] * start + pq[1, j] * end
        for h in range(2):
            trans[h, pl.ds(j, 8, stride=16), :] = value[h]
    for h in range(2):
        out_ref[128 * h : 128 * h + 128, :] = trans[h].T

    for copy in halo + halo_x + near_copies + far_copies:
        copy.wait_send()


def local(thermal_field, material_state, beam_path_indicator, state_diffusivity_table):
    f32 = jnp.float32
    flat = (256, 128)
    hbm = pl.BlockSpec(memory_space=pltpu.HBM)
    dma = pltpu.SemaphoreType.DMA
    out = pl.pallas_call(
        kernel,
        out_shape=pltpu.VMEM(flat, f32),
        in_specs=[hbm] * 4,
        out_specs=pl.BlockSpec(memory_space=pltpu.VMEM),
        scratch_shapes=[
            pltpu.SMEM((3,), f32),
            pltpu.VMEM(flat, f32),
            pltpu.VMEM(flat, jnp.int32),
            pltpu.VMEM(flat, jnp.int32),
            pltpu.VMEM(flat, f32),
            pltpu.VMEM(flat, f32),
            pltpu.VMEM((2, 128, 128), f32),
            pltpu.VMEM((3, 16, 2, 8, 128), f32),
            pltpu.VMEM((14, 2, 8, 128), f32),
            pltpu.VMEM((2, 2, 8, 128), f32),
            pltpu.VMEM((2, 2, 8, 128), f32),
            pltpu.VMEM((2, 2, 128), f32),
            pltpu.VMEM((2, 2, 128), f32),
            pltpu.VMEM((7, 2, 128), f32),
            pltpu.VMEM((5, 2, 128), f32),
            pltpu.VMEM((len(NEAR), 5, 2, 128), f32),
            pltpu.VMEM((3, 5, 2, 128), f32),
            pltpu.VMEM((len(FAR), 5, 2, 128), f32),
            dma((4,)),
            dma((2,)),
            dma((2,)),
            dma((2,)),
            dma((2,)),
            dma((len(NEAR),)),
            dma((len(NEAR),)),
            dma((len(FAR),)),
            dma((len(FAR),)),
        ],
        compiler_params=pltpu.CompilerParams(collective_id=0, has_side_effects=True),
        name="adi_x",
    )(
        thermal_field.reshape(flat),
        material_state.reshape(flat),
        beam_path_indicator.reshape(flat),
        state_diffusivity_table,
    )
    return out.reshape(thermal_field.shape)


def solution(mesh):
    in_specs = (P(None, "gy", "gx"), P(None, "gy", "gx"), P(None, "gy", "gx"), P())
    out_specs = P(None, "gy", "gx")
    return jax.shard_map(local, mesh=mesh, in_specs=in_specs, out_specs=out_specs, check_vma=False)
```

```python
import jax
import jax.numpy as jnp
from jax import lax
from jax.experimental import pallas as pl
from jax.experimental.pallas import tpu as pltpu
from jax.sharding import PartitionSpec as P

MESH = pl.DeviceIdType.MESH
RATIO = 65536.0
NSEG = 64
NGY = 8
NEAR = (-4, -3, -2, -1, 1, 2, 3)
GREET = (-3, -2, -1, 1, 2, 16, 32, 48)
FAR = (4, 12, 20, 28, 36, 44, 52, 60)


def face(a, b):
    return 2.0 * a * b / (a + b)


def split(x):
    high = 4097.0 * x
    high = high - (high - x)
    return high, x - high


def exact_face(a, b):
    above, below = 2.0 * a * b, a + b
    q = above / below
    (qh, ql), (bh, bl) = split(q), split(below)
    p = q * below
    error = ((qh * bh - p) + qh * bl + ql * bh) + ql * bl
    return q + ((above - p) - error) / below


def shunt_of(left, right):
    once = 1.0 + left
    diag = once + right
    part = diag - once
    return (once - left) - ((once - (diag - part)) + (right - part))


def combine(a, b):
    ab, aal, abe, as1, as2 = a
    bb, bal, bbe, bs1, bs2 = b
    shunt = abe + bal
    r = 1.0 / (ab + bb + shunt)
    pa, pb = ab * r, bb * r
    s = as2 + bs1
    return (pa * bb, aal + pa * shunt, bbe + pb * shunt, as1 + pa * s, bs2 + pb * s)


def build(g, shunts, lo, hi):
    if hi - lo == 1:
        return (g[lo], shunts[lo], None), []
    half = 1
    while half * 2 < hi - lo:
        half *= 2
    mid = lo + half
    (ab, aal, abe), left = build(g, shunts, lo, mid)
    (bb, bal, bbe), right = build(g, shunts, mid, hi)
    shunt = bal if abe is None else bal + abe
    r = 1.0 / (ab + bb + shunt)
    pa, pb = ab * r, bb * r
    al = aal + pa * shunt
    be = pb * shunt if bbe is None else bbe + pb * shunt
    return (pa * bb, al, be), left + right + [(mid, lo, hi, pa, pb, r)]


def kernel(
    t_hbm, m_hbm, b_hbm, table_hbm, out_ref,
    table, tv, mv, bv, cv, fv, trans, pq, elim, hs, hr, xs, xr, own, mine, near, mid, far,
    load_sem, hs_sem, hr_sem, xs_sem, xr_sem, ns_sem, nr_sem, fs_sem, fr_sem,
):
    gx, gy = lax.axis_index("gx"), lax.axis_index("gy")

    def seg(offset):
        return {"gx": lax.rem(gx + (offset % NSEG), NSEG)}

    def side(offset):
        return {"gy": lax.rem(gy + (offset % NGY), NGY)}

    barrier = pltpu.get_barrier_semaphore()
    greeted = [seg(o) for o in GREET]
    has = (gy > 0, gy < NGY - 1)
    for k in range(2):

        @pl.when(has[k])
        def _():
            pl.semaphore_signal(barrier, inc=1, device_id=side(2 * k - 1), device_id_type=MESH)

    for device in greeted:
        pl.semaphore_signal(barrier, inc=1, device_id=device, device_id_type=MESH)
    met = len(greeted) + jnp.where(has[0], 1, 0) + jnp.where(has[1], 1, 0)

    loads = [
        pltpu.make_async_copy(src, dst, load_sem.at[k])
        for k, (src, dst) in enumerate(((table_hbm, table), (m_hbm, mv), (t_hbm, tv), (b_hbm, bv)))
    ]
    for load in loads:
        load.start()
    loads[0].wait()
    t0, t1, t2 = table[0], table[1], table[2]

    def conductivity(m):
        return jnp.where(m == 0, t0, jnp.where(m == 1, t1, t2))

    low, high = pl.ds(0, 8, stride=32), pl.ds(31, 8, stride=32)
    loads[1].wait()
    hs[0, 1] = conductivity(mv[low, :])
    hs[1, 1] = conductivity(mv[high, :])
    loads[2].wait()
    hs[0, 0] = tv[low, :]
    hs[1, 0] = tv[high, :]

    pl.semaphore_wait(barrier, met)
    halo = [
        pltpu.make_async_remote_copy(
            src_ref=hs.at[k], dst_ref=hr.at[1 - k], send_sem=hs_sem.at[k], recv_sem=hr_sem.at[1 - k],
            device_id=side(2 * k - 1), device_id_type=MESH,
        )
        for k in range(2)
    ]
    for k in range(2):
        pl.when(has[k])(halo[k].start)
    cv[...] = conductivity(mv[...])
    for h in range(2):
        trans[h] = cv[128 * h : 128 * h + 128, :].T
        xs[0, h : h + 1, :] = trans[h, 0:1, :]
        xs[1, h : h + 1, :] = trans[h, 127:128, :]

    halo_x = [
        pltpu.make_async_remote_copy(
            src_ref=xs.at[k], dst_ref=xr.at[1 - k], send_sem=xs_sem.at[k], recv_sem=xr_sem.at[1 - k],
            device_id=seg(2 * k - 1), device_id_type=MESH,
        )
        for k in range(2)
    ]
    for copy in halo_x:
        copy.start()

    shape = (2, 8, 128)
    row = lax.broadcasted_iota(jnp.int32, shape, 1)

    tables = [jnp.full((8, 128), t, jnp.float32) for t in (t0, t1, t2)]
    faces = {}
    for i in range(3):
        for j in range(i, 3):
            faces[i, j] = faces[j, i] = RATIO * exact_face(tables[i], tables[j])[0:1, :]

    def joint(a, b):
        b0, b1 = b == t0, b == t1
        rows = [jnp.where(b0, faces[i, 0], jnp.where(b1, faces[i, 1], faces[i, 2])) for i in range(3)]
        return jnp.where(a == t0, rows[0], jnp.where(a == t1, rows[1], rows[2]))

    def piece(j):
        return jnp.stack([trans[h, pl.ds(j, 8, stride=16), :] for h in range(2)])

    cond = [piece(j) for j in range(16)]
    cond.append(pltpu.roll(cond[0], 7, 1))
    g = [joint(cond[j], cond[j + 1]) for j in range(16)]
    last = row == 7
    shunts = [jnp.where(row == 0, 0.0, shunt_of(pltpu.roll(g[15], 1, 1), g[0]))]
    shunts += [shunt_of(g[j - 1], g[j]) for j in range(1, 16)]
    (cb, cal, cbe), steps = build(g, shunts, 0, 15)
    cbe = cbe + jnp.where(last, 0.0, shunts[15])
    r15 = 1.0 / (cb + cbe + g[15])
    pa15, pb15 = cb * r15, g[15] * r15
    b = jnp.where(last, cb, pa15 * g[15])
    al = jnp.where(last, cal, cal + pa15 * cbe)
    be = jnp.where(last, cbe, pb15 * cbe)
    levels = []
    for step in (1, 2, 4):
        bb, bal, bbe = (pltpu.roll(v, 8 - step, 1) for v in (b, al, be))
        shunt = be + bal
        r = 1.0 / (b + bb + shunt)
        pa, pb = b * r, bb * r
        b, al, be = pa * bb, al + pa * shunt, bbe + pb * shunt
        levels.append((step, pa, pb, r))
    for h in range(2):
        own[0, h : h + 1, :] = b[h, 0:1, :]
        own[1, h : h + 1, :] = al[h, 0:1, :]
        own[2, h : h + 1, :] = be[h, 0:1, :]
        own[5, h : h + 1, :] = g[0][h, 0:1, :]
        own[6, h : h + 1, :] = g[14][h, 7:8, :]

    def spread(value, step):
        if step == 4:
            return jnp.broadcast_to(value[:, 0:1, :], shape)
        if step == 2:
            return jnp.where(row < 4, value[:, 0:1, :], value[:, 4:5, :])
        return jnp.where(row % 2 == 0, value, pltpu.roll(value, 1, 1))

    def descend(left, right, sources):
        for k, (step, pa, pb, _) in reversed(list(enumerate(levels))):
            centre = pa * left + pb * right
            if sources is not None:
                centre = centre + sources[0][k]
            centre = spread(centre, step)
            low = (row // step) % 2 == 0
            left, right = jnp.where(low, left, centre), jnp.where(low, centre, right)
        end = pa15 * left + pb15 * right
        if sources is not None:
            end = end + sources[1]
        values = {0: left, 15: jnp.where(last, right, end)}
        for node, lo, hi, pa, pb, _ in reversed(steps):
            values[node] = pa * values[lo] + pb * values[hi]
            if sources is not None:
                values[node] = values[node] + sources[2][node]
        return [values[j] for j in range(16)]

    one, zero = jnp.ones(shape, jnp.float32), jnp.zeros(shape, jnp.float32)
    for j, value in enumerate(descend(one, zero, None)):
        pq[0, j] = value
    for j, value in enumerate(descend(zero, one, None)):
        pq[1, j] = value
    for k, (_, _, _, _, _, r) in enumerate(steps):
        elim[k] = r

    loads[3].wait()
    line = lax.broadcasted_iota(jnp.int32, (32, 128), 0)
    below = None
    for z in range(8):
        here = slice(32 * z, 32 * z + 32)
        tz, cz = tv[here, :], cv[here, :]
        flux = jnp.where(line < 31, face(cz, pltpu.roll(cz, 31, 0)) * (pltpu.roll(tz, 31, 0) - tz), 0.0)
        value = tz + (flux - pltpu.roll(flux, 1, 0)) + 4.0 * bv[here, :].astype(jnp.float32)
        if below is not None:
            value = value - below
        if z < 7:
            above = slice(32 * z + 32, 32 * z + 64)
            below = face(cz, cv[above, :]) * (tv[above, :] - tz)
            value = value + below
        fv[here, :] = value

    for k in range(2):
        pl.when(has[1 - k])(halo[k].wait_recv)
    flux = face(hs[1, 1], hr[1, 1]) * (hr[1, 0] - hs[1, 0])
    fv[high, :] = fv[high, :] + jnp.where(gy < NGY - 1, flux, 0.0)
    flux = face(hs[0, 1], hr[0, 1]) * (hs[0, 0] - hr[0, 0])
    fv[low, :] = fv[low, :] - jnp.where(gy > 0, flux, 0.0)
    for h in range(2):
        trans[h] = fv[128 * h : 128 * h + 128, :].T

    first, second = zero, zero
    for j in range(16):
        f = piece(j)
        first, second = first + pq[0, j] * f, second + pq[1, j] * f
    for h in range(2):
        own[3, h : h + 1, :] = jnp.sum(first[h], axis=0, keepdims=True)
        own[4, h : h + 1, :] = jnp.sum(second[h], axis=0, keepdims=True)

    for copy in halo_x:
        copy.wait_recv()
    ob, oal, obe, os1, os2, first_g, last_g = (own[k] for k in range(7))
    og = jnp.where(gx < NSEG - 1, joint(xs[1], xr[1]), 0.0)
    oal = oal + shunt_of(jnp.where(gx > 0, joint(xr[0], xs[0]), 0.0), first_g)
    obe = obe + shunt_of(last_g, og)
    r = 1.0 / (ob + obe + og)
    pa, pb = ob * r, og * r
    whole = (pa * og, oal + pa * obe, pb * obe, os1 + pa * os2, pb * os2)
    for k in range(5):
        mine[k] = whole[k]
    near_copies = [
        pltpu.make_async_remote_copy(
            src_ref=mine, dst_ref=near.at[k], send_sem=ns_sem.at[k], recv_sem=nr_sem.at[k],
            device_id=seg(-o), device_id_type=MESH,
        )
        for k, o in enumerate(NEAR)
    ]
    for k in (0, 1, 6, 2, 5, 3, 4):
        near_copies[k].start()

    steps = [(node, lo, hi, pa, pb, elim[k]) for k, (node, lo, hi, pa, pb, _) in enumerate(steps)]
    f = [piece(j) for j in range(16)]
    ends = {(j, j + 1): (f[j], None) for j in range(15)}
    inner = {}
    for node, lo, hi, pa, pb, r in steps:
        a, c = ends[lo, node], ends[node, hi]
        s = c[0] if a[1] is None else a[1] + c[0]
        inner[node] = s * r
        ends[lo, hi] = (a[0] + pa * s, pb * s if c[1] is None else c[1] + pb * s)
    s1, s2 = ends[0, 15]
    s2 = s2 + f[15]
    at_end = r15 * s2
    s1, s2 = jnp.where(last, s1, s1 + pa15 * s2), jnp.where(last, s2, pb15 * s2)
    middle = []
    for step, pa, pb, r in levels:
        bs1, bs2 = pltpu.roll(s1, 8 - step, 1), pltpu.roll(s2, 8 - step, 1)
        s = s2 + bs1
        middle.append(s * r)
        s1, s2 = s1 + pa * s, bs2 + pb * s
    for j, value in enumerate(descend(zero, zero, (middle, at_end, inner))):
        pq[2, j] = value

    for copy in near_copies:
        copy.wait_recv()
    item = {o: tuple(near[k, i] for i in range(5)) for k, o in enumerate(NEAR)}
    item[0] = whole
    behind = combine(combine(item[-4], item[-3]), combine(item[-2], item[-1]))
    ahead = combine(item[2], item[3])
    own_ahead = combine(combine(item[0], item[1]), ahead)
    ahead = combine(item[1], ahead)
    window = combine(behind, own_ahead)
    for k in range(5):
        mid[0, k] = own_ahead[k]
        mid[1, k] = window[k]
        mid[2, k] = behind[k]
    far_copies = [
        pltpu.make_async_remote_copy(
            src_ref=mid.at[0 if k == 0 else 2 if k == 7 else 1], dst_ref=far.at[k],
            send_sem=fs_sem.at[k], recv_sem=fr_sem.at[k],
            device_id=seg(-o), device_id_type=MESH,
        )
        for k, o in enumerate(FAR)
    ]
    for k in (3, 4, 2, 5, 1, 6, 0, 7):
        far_copies[k].start()
    for copy in far_copies:
        copy.wait_recv()
    chain = [ahead] + [tuple(far[k, i] for i in range(5)) for k in range(8)] + [behind]
    while len(chain) > 1:
        chain = [combine(*chain[k : k + 2]) if k + 1 < len(chain) else chain[k] for k in range(0, len(chain), 2)]
    _, right_g, left_g, right_s, left_s = chain[0]

    r = og / (og + right_g)
    end_g, end_s = obe + r * right_g, os2 + r * right_s
    r = 1.0 / (ob + end_g)
    start = (os1 + left_s + ob * r * end_s) / (oal + left_g + ob * r * end_g)
    end = r * (ob * start + end_s)
    start = jnp.stack([jnp.broadcast_to(start[h : h + 1, :], (8, 128)) for h in range(2)])
    end = jnp.stack([jnp.broadcast_to(end[h : h + 1, :], (8, 128)) for h in range(2)])
    for j in range(16):
        value = pq[2, j] + pq[0, j] * start + pq[1, j] * end
        for h in range(2):
            trans[h, pl.ds(j, 8, stride=16), :] = value[h]
    for h in range(2):
        out_ref[128 * h : 128 * h + 128, :] = trans[h].T

    for k in range(2):
        pl.when(has[k])(halo[k].wait_send)
    for copy in halo_x + near_copies + far_copies:
        copy.wait_send()


def local(thermal_field, material_state, beam_path_indicator, state_diffusivity_table):
    f32 = jnp.float32
    flat = (256, 128)
    hbm = pl.BlockSpec(memory_space=pltpu.HBM)
    dma = pltpu.SemaphoreType.DMA
    out = pl.pallas_call(
        kernel,
        out_shape=pltpu.VMEM(flat, f32),
        in_specs=[hbm] * 4,
        out_specs=pl.BlockSpec(memory_space=pltpu.VMEM),
        scratch_shapes=[
            pltpu.SMEM((3,), f32),
            pltpu.VMEM(flat, f32),
            pltpu.VMEM(flat, jnp.int32),
            pltpu.VMEM(flat, jnp.int32),
            pltpu.VMEM(flat, f32),
            pltpu.VMEM(flat, f32),
            pltpu.VMEM((2, 128, 128), f32),
            pltpu.VMEM((3, 16, 2, 8, 128), f32),
            pltpu.VMEM((14, 2, 8, 128), f32),
            pltpu.VMEM((2, 2, 8, 128), f32),
            pltpu.VMEM((2, 2, 8, 128), f32),
            pltpu.VMEM((2, 2, 128), f32),
            pltpu.VMEM((2, 2, 128), f32),
            pltpu.VMEM((7, 2, 128), f32),
            pltpu.VMEM((5, 2, 128), f32),
            pltpu.VMEM((len(NEAR), 5, 2, 128), f32),
            pltpu.VMEM((3, 5, 2, 128), f32),
            pltpu.VMEM((len(FAR), 5, 2, 128), f32),
            dma((4,)),
            dma((2,)),
            dma((2,)),
            dma((2,)),
            dma((2,)),
            dma((len(NEAR),)),
            dma((len(NEAR),)),
            dma((len(FAR),)),
            dma((len(FAR),)),
        ],
        compiler_params=pltpu.CompilerParams(collective_id=0, has_side_effects=True),
        name="adi_x",
    )(
        thermal_field.reshape(flat),
        material_state.reshape(flat),
        beam_path_indicator.reshape(flat),
        state_diffusivity_table,
    )
    return out.reshape(thermal_field.shape)


def solution(mesh):
    in_specs = (P(None, "gy", "gx"), P(None, "gy", "gx"), P(None, "gy", "gx"), P())
    out_specs = P(None, "gy", "gx")
    return jax.shard_map(local, mesh=mesh, in_specs=in_specs, out_specs=out_specs, check_vma=False)
```

```python
import jax
import jax.numpy as jnp
from jax import lax
from jax.experimental import pallas as pl
from jax.experimental.pallas import tpu as pltpu
from jax.sharding import PartitionSpec as P

MESH = pl.DeviceIdType.MESH
RATIO = 65536.0
NSEG = 64
NGY = 8
NEAR = (-4, -3, -2, -1, 1, 2, 3)
GREET = (-2, -1, 1, 2, 16, 32, 48)
FAR = (4, 12, 20, 28, 36, 44, 52, 60)


def face(a, b):
    return 2.0 * a * b / (a + b)


def split(x):
    high = 4097.0 * x
    high = high - (high - x)
    return high, x - high


def exact_face(a, b):
    above, below = 2.0 * a * b, a + b
    q = above / below
    (qh, ql), (bh, bl) = split(q), split(below)
    p = q * below
    error = ((qh * bh - p) + qh * bl + ql * bh) + ql * bl
    return q + ((above - p) - error) / below


def shunt_of(left, right):
    once = 1.0 + left
    diag = once + right
    part = diag - once
    return (once - left) - ((once - (diag - part)) + (right - part))


def combine(a, b):
    ab, aal, abe, as1, as2 = a
    bb, bal, bbe, bs1, bs2 = b
    shunt = abe + bal
    r = 1.0 / (ab + bb + shunt)
    pa, pb = ab * r, bb * r
    s = as2 + bs1
    return (pa * bb, aal + pa * shunt, bbe + pb * shunt, as1 + pa * s, bs2 + pb * s)


def build(g, shunts, lo, hi):
    if hi - lo == 1:
        return (g[lo], shunts[lo], None), []
    half = 1
    while half * 2 < hi - lo:
        half *= 2
    mid = lo + half
    (ab, aal, abe), left = build(g, shunts, lo, mid)
    (bb, bal, bbe), right = build(g, shunts, mid, hi)
    shunt = bal if abe is None else bal + abe
    r = 1.0 / (ab + bb + shunt)
    pa, pb = ab * r, bb * r
    al = aal + pa * shunt
    be = pb * shunt if bbe is None else bbe + pb * shunt
    return (pa * bb, al, be), left + right + [(mid, lo, hi, pa, pb, r)]


def kernel(
    t_hbm, m_hbm, b_hbm, table_hbm, out_ref,
    table, tv, mv, bv, cv, fv, trans, pq, elim, hs, hr, xs, xr, own, mine, near, mid, far,
    load_sem, hs_sem, hr_sem, xs_sem, xr_sem, ns_sem, nr_sem, fs_sem, fr_sem, word_sem,
):
    gx, gy = lax.axis_index("gx"), lax.axis_index("gy")

    def seg(offset):
        return {"gx": lax.rem(gx + (offset % NSEG), NSEG)}

    def side(offset):
        return {"gy": lax.rem(gy + (offset % NGY), NGY)}

    barrier = pltpu.get_barrier_semaphore()
    greeted = [side(1), side(-1)] + [seg(o) for o in GREET]
    for device in greeted:
        pl.semaphore_signal(barrier, inc=1, device_id=device, device_id_type=MESH)

    loads = [
        pltpu.make_async_copy(src, dst, load_sem.at[k])
        for k, (src, dst) in enumerate(((table_hbm, table), (m_hbm, mv), (t_hbm, tv), (b_hbm, bv)))
    ]
    for load in loads:
        load.start()
    loads[0].wait()
    t0, t1, t2 = table[0], table[1], table[2]

    def conductivity(m):
        return jnp.where(m == 0, t0, jnp.where(m == 1, t1, t2))

    low, high = pl.ds(0, 8, stride=32), pl.ds(31, 8, stride=32)
    loads[1].wait()
    hs[0, 1] = conductivity(mv[low, :])
    hs[1, 1] = conductivity(mv[high, :])
    loads[2].wait()
    hs[0, 0] = tv[low, :]
    hs[1, 0] = tv[high, :]

    cv[...] = conductivity(mv[...])
    for h in range(2):
        trans[h] = cv[128 * h : 128 * h + 128, :].T
        xs[0, h : h + 1, :] = trans[h, 0:1, :]
        xs[1, h : h + 1, :] = trans[h, 127:128, :]
    pl.semaphore_wait(barrier, len(greeted))
    for k in range(2):
        pl.semaphore_signal(word_sem.at[k], inc=1, device_id=seg(4 * k - 2), device_id_type=MESH)

    halo = [
        pltpu.make_async_remote_copy(
            src_ref=hs.at[k], dst_ref=hr.at[1 - k], send_sem=hs_sem.at[k], recv_sem=hr_sem.at[1 - k],
            device_id=side(2 * k - 1), device_id_type=MESH,
        )
        for k in range(2)
    ]
    for copy in halo:
        copy.start()

    halo_x = [
        pltpu.make_async_remote_copy(
            src_ref=xs.at[k], dst_ref=xr.at[1 - k], send_sem=xs_sem.at[k], recv_sem=xr_sem.at[1 - k],
            device_id=seg(2 * k - 1), device_id_type=MESH,
        )
        for k in range(2)
    ]
    for copy in halo_x:
        copy.start()

    shape = (2, 8, 128)
    row = lax.broadcasted_iota(jnp.int32, shape, 1)

    tables = [jnp.full((8, 128), t, jnp.float32) for t in (t0, t1, t2)]
    faces = {}
    for i in range(3):
        for j in range(i, 3):
            faces[i, j] = faces[j, i] = RATIO * exact_face(tables[i], tables[j])[0:1, :]

    def joint(a, b):
        b0, b1 = b == t0, b == t1
        rows = [jnp.where(b0, faces[i, 0], jnp.where(b1, faces[i, 1], faces[i, 2])) for i in range(3)]
        return jnp.where(a == t0, rows[0], jnp.where(a == t1, rows[1], rows[2]))

    def piece(j):
        return jnp.stack([trans[h, pl.ds(j, 8, stride=16), :] for h in range(2)])

    cond = [piece(j) for j in range(16)]
    cond.append(pltpu.roll(cond[0], 7, 1))
    g = [joint(cond[j], cond[j + 1]) for j in range(16)]
    last = row == 7
    shunts = [jnp.where(row == 0, 0.0, shunt_of(pltpu.roll(g[15], 1, 1), g[0]))]
    shunts += [shunt_of(g[j - 1], g[j]) for j in range(1, 16)]
    (cb, cal, cbe), steps = build(g, shunts, 0, 15)
    cbe = cbe + jnp.where(last, 0.0, shunts[15])
    r15 = 1.0 / (cb + cbe + g[15])
    pa15, pb15 = cb * r15, g[15] * r15
    b = jnp.where(last, cb, pa15 * g[15])
    al = jnp.where(last, cal, cal + pa15 * cbe)
    be = jnp.where(last, cbe, pb15 * cbe)
    levels = []
    for step in (1, 2, 4):
        bb, bal, bbe = (pltpu.roll(v, 8 - step, 1) for v in (b, al, be))
        shunt = be + bal
        r = 1.0 / (b + bb + shunt)
        pa, pb = b * r, bb * r
        b, al, be = pa * bb, al + pa * shunt, bbe + pb * shunt
        levels.append((step, pa, pb, r))
    for h in range(2):
        own[0, h : h + 1, :] = b[h, 0:1, :]
        own[1, h : h + 1, :] = al[h, 0:1, :]
        own[2, h : h + 1, :] = be[h, 0:1, :]
        own[5, h : h + 1, :] = g[0][h, 0:1, :]
        own[6, h : h + 1, :] = g[14][h, 7:8, :]

    def spread(value, step):
        if step == 4:
            return jnp.broadcast_to(value[:, 0:1, :], shape)
        if step == 2:
            return jnp.where(row < 4, value[:, 0:1, :], value[:, 4:5, :])
        return jnp.where(row % 2 == 0, value, pltpu.roll(value, 1, 1))

    def descend(left, right, sources):
        for k, (step, pa, pb, _) in reversed(list(enumerate(levels))):
            centre = pa * left + pb * right
            if sources is not None:
                centre = centre + sources[0][k]
            centre = spread(centre, step)
            low = (row // step) % 2 == 0
            left, right = jnp.where(low, left, centre), jnp.where(low, centre, right)
        end = pa15 * left + pb15 * right
        if sources is not None:
            end = end + sources[1]
        values = {0: left, 15: jnp.where(last, right, end)}
        for node, lo, hi, pa, pb, _ in reversed(steps):
            values[node] = pa * values[lo] + pb * values[hi]
            if sources is not None:
                values[node] = values[node] + sources[2][node]
        return [values[j] for j in range(16)]

    one, zero = jnp.ones(shape, jnp.float32), jnp.zeros(shape, jnp.float32)
    for j, value in enumerate(descend(one, zero, None)):
        pq[0, j] = value
    for j, value in enumerate(descend(zero, one, None)):
        pq[1, j] = value
    for k, (_, _, _, _, _, r) in enumerate(steps):
        elim[k] = r

    loads[3].wait()
    line = lax.broadcasted_iota(jnp.int32, (32, 128), 0)
    below = None
    for z in range(8):
        here = slice(32 * z, 32 * z + 32)
        tz, cz = tv[here, :], cv[here, :]
        flux = jnp.where(line < 31, face(cz, pltpu.roll(cz, 31, 0)) * (pltpu.roll(tz, 31, 0) - tz), 0.0)
        value = tz + (flux - pltpu.roll(flux, 1, 0)) + 4.0 * bv[here, :].astype(jnp.float32)
        if below is not None:
            value = value - below
        if z < 7:
            above = slice(32 * z + 32, 32 * z + 64)
            below = face(cz, cv[above, :]) * (tv[above, :] - tz)
            value = value + below
        fv[here, :] = value

    for copy in halo:
        copy.wait_recv()
    flux = face(hs[1, 1], hr[1, 1]) * (hr[1, 0] - hs[1, 0])
    fv[high, :] = fv[high, :] + jnp.where(gy < NGY - 1, flux, 0.0)
    flux = face(hs[0, 1], hr[0, 1]) * (hs[0, 0] - hr[0, 0])
    fv[low, :] = fv[low, :] - jnp.where(gy > 0, flux, 0.0)
    for h in range(2):
        trans[h] = fv[128 * h : 128 * h + 128, :].T

    first, second = zero, zero
    for j in range(16):
        f = piece(j)
        first, second = first + pq[0, j] * f, second + pq[1, j] * f
    for h in range(2):
        own[3, h : h + 1, :] = jnp.sum(first[h], axis=0, keepdims=True)
        own[4, h : h + 1, :] = jnp.sum(second[h], axis=0, keepdims=True)

    for copy in halo_x:
        copy.wait_recv()
    ob, oal, obe, os1, os2, first_g, last_g = (own[k] for k in range(7))
    og = jnp.where(gx < NSEG - 1, joint(xs[1], xr[1]), 0.0)
    oal = oal + shunt_of(jnp.where(gx > 0, joint(xr[0], xs[0]), 0.0), first_g)
    obe = obe + shunt_of(last_g, og)
    r = 1.0 / (ob + obe + og)
    pa, pb = ob * r, og * r
    whole = (pa * og, oal + pa * obe, pb * obe, os1 + pa * os2, pb * os2)
    for k in range(5):
        mine[k] = whole[k]
    near_copies = [
        pltpu.make_async_remote_copy(
            src_ref=mine, dst_ref=near.at[k], send_sem=ns_sem.at[k], recv_sem=nr_sem.at[k],
            device_id=seg(-o), device_id_type=MESH,
        )
        for k, o in enumerate(NEAR)
    ]
    for k in (2, 3, 4):
        near_copies[k].start()
    for k in range(2):
        pl.semaphore_wait(word_sem.at[k], 1)
    for k in (0, 1, 6, 5):
        near_copies[k].start()

    steps = [(node, lo, hi, pa, pb, elim[k]) for k, (node, lo, hi, pa, pb, _) in enumerate(steps)]
    f = [piece(j) for j in range(16)]
    ends = {(j, j + 1): (f[j], None) for j in range(15)}
    inner = {}
    for node, lo, hi, pa, pb, r in steps:
        a, c = ends[lo, node], ends[node, hi]
        s = c[0] if a[1] is None else a[1] + c[0]
        inner[node] = s * r
        ends[lo, hi] = (a[0] + pa * s, pb * s if c[1] is None else c[1] + pb * s)
    s1, s2 = ends[0, 15]
    s2 = s2 + f[15]
    at_end = r15 * s2
    s1, s2 = jnp.where(last, s1, s1 + pa15 * s2), jnp.where(last, s2, pb15 * s2)
    middle = []
    for step, pa, pb, r in levels:
        bs1, bs2 = pltpu.roll(s1, 8 - step, 1), pltpu.roll(s2, 8 - step, 1)
        s = s2 + bs1
        middle.append(s * r)
        s1, s2 = s1 + pa * s, bs2 + pb * s
    for j, value in enumerate(descend(zero, zero, (middle, at_end, inner))):
        pq[2, j] = value

    for copy in near_copies:
        copy.wait_recv()
    item = {o: tuple(near[k, i] for i in range(5)) for k, o in enumerate(NEAR)}
    item[0] = whole
    behind = combine(combine(item[-4], item[-3]), combine(item[-2], item[-1]))
    ahead = combine(item[2], item[3])
    own_ahead = combine(combine(item[0], item[1]), ahead)
    ahead = combine(item[1], ahead)
    window = combine(behind, own_ahead)
    for k in range(5):
        mid[0, k] = own_ahead[k]
        mid[1, k] = window[k]
        mid[2, k] = behind[k]
    far_copies = [
        pltpu.make_async_remote_copy(
            src_ref=mid.at[0 if k == 0 else 2 if k == 7 else 1], dst_ref=far.at[k],
            send_sem=fs_sem.at[k], recv_sem=fr_sem.at[k],
            device_id=seg(-o), device_id_type=MESH,
        )
        for k, o in enumerate(FAR)
    ]
    for k in (3, 4, 2, 5, 1, 6, 0, 7):
        far_copies[k].start()
    def arrived(k):
        far_copies[k].wait_recv()
        return tuple(far[k, i] for i in range(5))

    head = combine(combine(ahead, arrived(0)), combine(arrived(1), arrived(2)))
    tail = combine(arrived(6), combine(arrived(7), behind))
    centre = combine(combine(arrived(3), arrived(4)), arrived(5))
    _, right_g, left_g, right_s, left_s = combine(combine(head, centre), tail)

    r = og / (og + right_g)
    end_g, end_s = obe + r * right_g, os2 + r * right_s
    r = 1.0 / (ob + end_g)
    start = (os1 + left_s + ob * r * end_s) / (oal + left_g + ob * r * end_g)
    end = r * (ob * start + end_s)
    start = jnp.stack([jnp.broadcast_to(start[h : h + 1, :], (8, 128)) for h in range(2)])
    end = jnp.stack([jnp.broadcast_to(end[h : h + 1, :], (8, 128)) for h in range(2)])
    for j in range(16):
        value = pq[2, j] + pq[0, j] * start + pq[1, j] * end
        for h in range(2):
            trans[h, pl.ds(j, 8, stride=16), :] = value[h]
    for h in range(2):
        out_ref[128 * h : 128 * h + 128, :] = trans[h].T

    for copy in halo + halo_x + near_copies + far_copies:
        copy.wait_send()


def local(thermal_field, material_state, beam_path_indicator, state_diffusivity_table):
    f32 = jnp.float32
    flat = (256, 128)
    hbm = pl.BlockSpec(memory_space=pltpu.HBM)
    dma = pltpu.SemaphoreType.DMA
    out = pl.pallas_call(
        kernel,
        out_shape=pltpu.VMEM(flat, f32),
        in_specs=[hbm] * 4,
        out_specs=pl.BlockSpec(memory_space=pltpu.VMEM),
        scratch_shapes=[
            pltpu.SMEM((3,), f32),
            pltpu.VMEM(flat, f32),
            pltpu.VMEM(flat, jnp.int32),
            pltpu.VMEM(flat, jnp.int32),
            pltpu.VMEM(flat, f32),
            pltpu.VMEM(flat, f32),
            pltpu.VMEM((2, 128, 128), f32),
            pltpu.VMEM((3, 16, 2, 8, 128), f32),
            pltpu.VMEM((14, 2, 8, 128), f32),
            pltpu.VMEM((2, 2, 8, 128), f32),
            pltpu.VMEM((2, 2, 8, 128), f32),
            pltpu.VMEM((2, 2, 128), f32),
            pltpu.VMEM((2, 2, 128), f32),
            pltpu.VMEM((7, 2, 128), f32),
            pltpu.VMEM((5, 2, 128), f32),
            pltpu.VMEM((len(NEAR), 5, 2, 128), f32),
            pltpu.VMEM((3, 5, 2, 128), f32),
            pltpu.VMEM((len(FAR), 5, 2, 128), f32),
            dma((4,)),
            dma((2,)),
            dma((2,)),
            dma((2,)),
            dma((2,)),
            dma((len(NEAR),)),
            dma((len(NEAR),)),
            dma((len(FAR),)),
            dma((len(FAR),)),
            pltpu.SemaphoreType.REGULAR((2,)),
        ],
        compiler_params=pltpu.CompilerParams(collective_id=0, has_side_effects=True),
        name="adi_x",
    )(
        thermal_field.reshape(flat),
        material_state.reshape(flat),
        beam_path_indicator.reshape(flat),
        state_diffusivity_table,
    )
    return out.reshape(thermal_field.shape)


def solution(mesh):
    in_specs = (P(None, "gy", "gx"), P(None, "gy", "gx"), P(None, "gy", "gx"), P())
    out_specs = P(None, "gy", "gx")
    return jax.shard_map(local, mesh=mesh, in_specs=in_specs, out_specs=out_specs, check_vma=False)
```
